32 devices in a mesh: groups: 2 (over y), ctx: 16 (over z, x, core).
Axes of the slice: x: 2, y: 2, z: 4, core: 2. Of those that a mesh axis runs over, the one named last changes fastest.
Arguments:
- softmax_query: bfloat16 [4096, 512], P(('groups', 'ctx')), parts along dimension 0, may hold values from -90 to 90
- softmax_key: bfloat16 [4096, 128], P(('groups', 'ctx')), parts along dimension 0, may hold values from -6 to 6
- softmax_value: bfloat16 [4096, 128], P(('groups', 'ctx')), parts along dimension 0, may hold values from -6 to 6
- softmax_output: bfloat16 [4096, 512], P(('groups', 'ctx')), parts along dimension 0, may hold values from -6 to 6
- upstream_grad: bfloat16 [4096, 512], P(('groups', 'ctx')), parts along dimension 0, may hold values from -6 to 6
- linear_query: bfloat16 [4096, 512], P(('groups', 'ctx')), parts along dimension 0, may hold values from -0.1796875 to 0.1796875
- linear_key: bfloat16 [4096, 512], P(('groups', 'ctx')), parts along dimension 0, may hold values from -0.1796875 to 0.1796875
- linear_value: bfloat16 [4096, 512], P(('groups', 'ctx')), parts along dimension 0, may hold values from -6 to 6
- linear_decay: float32 [4096, 4], P(('groups', 'ctx')), parts along dimension 0, may hold values from -1 to 0
- document_ids: int32 [4096], P('groups'), parts along dimension 0, may hold values from 0 to 3, never falling along the last dimension, each value on 1 to 1024 neighbouring positions
Outputs:
- key_gradient: bfloat16 [4096, 128], P(('groups', 'ctx')), parts along dimension 0
- value_gradient: bfloat16 [4096, 128], P(('groups', 'ctx')), parts along dimension 0
- query_cotangent: bfloat16 [4096, 512], P(('groups', 'ctx')), parts along dimension 0
- key_cotangent: bfloat16 [4096, 512], P(('groups', 'ctx')), parts along dimension 0
- value_cotangent: bfloat16 [4096, 512], P(('groups', 'ctx')), parts along dimension 0
The draws below stay inside these ranges and needn't reach their ends.
There are 2 independent parts, one for each index of `groups`. The reference program is written for one: setup_inputs(seed, part) draws one part's arguments, and reference() takes and returns one part's arrays. A program takes and returns all parts, laid end to end along the dimension named above; each array names one. Nothing has to cross between parts.
All inputs are finite; a program needn't handle non-finite values.
Results may differ from the reference program's by a relative error of at most 0.0051.
Values may be sent and summed in bfloat16 or wider, within the bound.
No kernel may reach another device: no remote copies, remote signals or barrier semaphores. Data moves between devices by JAX's collectives and lax.ppermute only.
A program may use at most 256 MiB of HBM per device.

```python
import math
import jax
import jax.numpy as jnp
import numpy as np
from jax import lax

DH = 128
ASKING_CHANNELS = 4
TOK_DEV = 128
DOCS = 4
TEXT_POSITIONS = 2048
FEAT = 512


def shared_draw(key):
    initial_number = jax.random.fold_in(key, 7)
    key_matrix = jnp.clip(jax.random.normal(jax.random.fold_in(initial_number, 1), (TEXT_POSITIONS, DH), jnp.float32), -6.0, 6.0)
    query = jnp.clip(jax.random.normal(jax.random.fold_in(initial_number, 2), (TEXT_POSITIONS, ASKING_CHANNELS * DH), jnp.float32), -6.0, 6.0)
    return (query, key_matrix)


def draw_softmax_query(key, part):
    return shared_draw(key)[0].astype(jnp.bfloat16)


def draw_softmax_key(key, part):
    return shared_draw(key)[1].astype(jnp.bfloat16)


def draw_linear_decay(key, part):
    initial_number = jax.random.fold_in(key, 11)
    low_end = math.log(0.5 / TEXT_POSITIONS)
    high_end = math.log(1.0 / 30.0)
    fading_speed = jnp.exp(jax.random.uniform(jax.random.fold_in(initial_number, 1), (1, ASKING_CHANNELS), jnp.float32, low_end, high_end))
    processor_factor = jnp.exp(jax.random.uniform(jax.random.fold_in(initial_number, 2), (TEXT_POSITIONS // TOK_DEV, ASKING_CHANNELS), jnp.float32, -0.7, 0.7))
    processor_factor = jnp.repeat(processor_factor, TOK_DEV, axis=0)
    rough_guess = jax.random.uniform(jax.random.fold_in(initial_number, 3), (TEXT_POSITIONS, ASKING_CHANNELS), jnp.float32, 0.5, 1.5)
    segment_opening = jax.random.uniform(jax.random.fold_in(initial_number, 4), (TEXT_POSITIONS, ASKING_CHANNELS), jnp.float32) < 6.0 / TEXT_POSITIONS
    segment_extent = jax.random.uniform(jax.random.fold_in(initial_number, 5), (TEXT_POSITIONS, ASKING_CHANNELS), jnp.float32, 0.22, 0.69)
    segment_lines = jnp.where(segment_opening, segment_extent, 0.0)
    return -(fading_speed * processor_factor * rough_guess) - segment_lines


def shard_levels(stream_key, dims, cuts, low, high):
    gain = 1.0
    for axis_at, shards_of in cuts:
        draws = jax.random.uniform(jax.random.fold_in(jax.random.fold_in(stream_key, 6), axis_at), (shards_of,), jnp.float32, low / len(cuts), high / len(cuts))
        gain = gain * jnp.repeat(jnp.exp(draws), dims[axis_at] // shards_of).reshape((-1,) + (1,) * (len(dims) - 1 - axis_at))
    return gain


def profile(number_of, total, limit, lean):
    portions = [(1 << 20) // math.isqrt(grade ** lean) + 1 for grade in range(2, number_of + 1)]
    surplus, given = total - limit - (number_of - 1), [1] * (number_of - 1)
    while surplus > 0:
        movable = [i for i in range(number_of - 1) if given[i] < limit]
        whole, remaining = sum([portions[i] for i in movable]), surplus
        for i in movable:
            extra = min(limit - given[i], max(1, remaining * portions[i] // whole), surplus)
            given[i] = given[i] + extra
            surplus = surplus - extra
    return np.array([limit] + given)


def uneven_parts(rng, number_of, total, reach, skew):
    if number_of == 2:
        one = jax.random.randint(rng, (), max(1, total - reach), min(reach, total - 1) + 1)
        return jnp.stack([one, total - one])
    sizes = jnp.asarray(profile(number_of, total, reach, skew), jnp.int32)
    twos = (number_of - 1) // 2
    source_of, taker = sizes[1:1 + 2 * twos:2], sizes[2:2 + 2 * twos:2]
    margin = jnp.minimum(source_of - 1, reach - taker)
    shifted = jax.random.randint(jax.random.fold_in(rng, 1), (twos,), 0, 1 << 20) % (margin + 1)
    sizes = sizes.at[1:1 + 2 * twos:2].set(source_of - shifted).at[2:2 + 2 * twos:2].set(taker + shifted)
    return sizes[jax.random.permutation(jax.random.fold_in(rng, 2), number_of)]


def bell_draw(key, shape, spread, bound, cuts=(), kind=jnp.bfloat16):
    level = shard_levels(key, shape, cuts, -0.22, 0.18) if cuts else 1.0
    values = jax.random.normal(key, shape, jnp.float32) * spread * level
    return jnp.minimum(jnp.maximum(values, -bound), bound).astype(kind)


def setup_inputs(seed: int = 0, part: int = 0) -> dict:
    seeds = jax.random.split(jax.random.key(seed), 11)
    own_keys = jax.random.split(jax.random.fold_in(seeds[10], part), 11)
    softmax_query = draw_softmax_query(jax.random.fold_in(jax.random.fold_in(seeds[10], part), 71), part)
    softmax_key = draw_softmax_key(jax.random.fold_in(jax.random.fold_in(seeds[10], part), 71), part)
    softmax_value = bell_draw(own_keys[2], (TEXT_POSITIONS, DH), 1.0, 6.0, ((0, 16),))
    softmax_output = bell_draw(own_keys[3], (TEXT_POSITIONS, FEAT), 1.0, 6.0, ((0, 16),))
    upstream_grad = bell_draw(own_keys[4], (TEXT_POSITIONS, FEAT), 1.0, 6.0, ((0, 16),))
    linear_query = bell_draw(own_keys[5], (TEXT_POSITIONS, FEAT), 0.03, 0.1796875, ((0, 16),))
    linear_key = bell_draw(own_keys[6], (TEXT_POSITIONS, FEAT), 0.03, 0.1796875, ((0, 16),))
    linear_value = bell_draw(own_keys[7], (TEXT_POSITIONS, FEAT), 1.0, 6.0, ((0, 16),))
    linear_decay = draw_linear_decay(jax.random.fold_in(jax.random.fold_in(seeds[10], part), 71), part)
    document_ids = jnp.searchsorted(jnp.cumsum(uneven_parts(own_keys[9], DOCS, TEXT_POSITIONS, TEXT_POSITIONS // 2, 2)), jnp.arange(TEXT_POSITIONS), side="right").astype(jnp.int32)
    return {"softmax_query": softmax_query, "softmax_key": softmax_key, "softmax_value": softmax_value, "softmax_output": softmax_output, "upstream_grad": upstream_grad, "linear_query": linear_query, "linear_key": linear_key, "linear_value": linear_value, "linear_decay": linear_decay, "document_ids": document_ids}


very_low = -1e30


def to_positions(array):
    shards = TEXT_POSITIONS // TOK_DEV
    rest = array.shape[1:]
    return array.reshape((shards, TOK_DEV) + rest).swapaxes(0, 1).reshape(array.shape)


def to_stripes(array):
    shards = TEXT_POSITIONS // TOK_DEV
    rest = array.shape[1:]
    return array.reshape((TOK_DEV, shards) + rest).swapaxes(0, 1).reshape(array.shape)


def round_low(array):
    return lax.optimization_barrier(array.astype(jnp.bfloat16)).astype(jnp.float32)


def softmax_part(softmax_query, softmax_key, softmax_value, softmax_output, upstream_grad, document_ids):
    score_scaling = DH ** -0.5
    block_rows = min(512, TEXT_POSITIONS)
    query = to_positions(softmax_query).reshape(TEXT_POSITIONS, ASKING_CHANNELS, DH).astype(jnp.float32)
    key_matrix = to_positions(softmax_key).astype(jnp.float32)
    value_matrix = to_positions(softmax_value).astype(jnp.float32)
    grads = to_positions(upstream_grad).reshape(TEXT_POSITIONS, ASKING_CHANNELS, DH).astype(jnp.float32)
    saved = to_positions(softmax_output).reshape(TEXT_POSITIONS, ASKING_CHANNELS, DH).astype(jnp.float32)
    row_delta = jnp.sum(grads * saved, axis=-1)
    positions = jnp.arange(TEXT_POSITIONS, dtype=jnp.int32)

    def one_block(carry, block_index):
        key_accumulator, value_accumulator = carry
        begin = (block_index * block_rows).astype(jnp.int32)
        query_tile_block = lax.dynamic_slice_in_dim(query, begin, block_rows, 0)
        gradient_block = lax.dynamic_slice_in_dim(grads, begin, block_rows, 0)
        delta_block = lax.dynamic_slice_in_dim(row_delta, begin, block_rows, 0)
        pos_block = lax.dynamic_slice_in_dim(positions, begin, block_rows, 0)
        doc_block = lax.dynamic_slice_in_dim(document_ids, begin, block_rows, 0)
        score_matrix = jnp.einsum("rjl,pl->rjp", query_tile_block, key_matrix) * score_scaling
        allowed = (positions[None, :] <= pos_block[:, None]) & (document_ids[None, :] == doc_block[:, None])
        allowed = allowed[:, None, :]
        row_max = jnp.max(jnp.where(allowed, score_matrix, very_low), axis=-1, keepdims=True)
        expo = jnp.where(allowed, jnp.exp(score_matrix - row_max), 0.0)
        probs = expo / jnp.sum(expo, axis=-1, keepdims=True)
        probability_gradient = jnp.einsum("rjl,pl->rjp", gradient_block, value_matrix)
        score_gradient = round_low(probs * (probability_gradient - delta_block[..., None]) * score_scaling)
        probability_reduced = round_low(probs)
        query_gradient = jnp.einsum("yrv,vg->yrg", score_gradient, key_matrix)
        stream = (gradient_block + query_gradient).astype(jnp.bfloat16)
        key_accumulator = key_accumulator + jnp.einsum("ghv,ghp->vp", score_gradient, query_tile_block)
        value_accumulator = value_accumulator + jnp.einsum("ghv,ghp->vp", probability_reduced, gradient_block)
        return (key_accumulator, value_accumulator), stream

    zeros = jnp.zeros((TEXT_POSITIONS, DH), jnp.float32)
    (key_accumulator, value_accumulator), streams = lax.scan(one_block, (zeros, zeros), jnp.arange(TEXT_POSITIONS // block_rows, dtype=jnp.int32))
    stream_grad = streams.reshape(TEXT_POSITIONS, ASKING_CHANNELS * DH)
    return to_stripes(key_accumulator).astype(jnp.bfloat16), to_stripes(value_accumulator).astype(jnp.bfloat16), stream_grad


def lightning_part(stream_grad, linear_query, linear_key, linear_value, linear_decay, document_ids):
    highest = lax.Precision.HIGHEST
    block_rows = min(512, TEXT_POSITIONS)
    query = linear_query.reshape(TEXT_POSITIONS, ASKING_CHANNELS, DH).astype(jnp.float32)
    key_matrix = linear_key.reshape(TEXT_POSITIONS, ASKING_CHANNELS, DH).astype(jnp.float32)
    value_matrix = linear_value.reshape(TEXT_POSITIONS, ASKING_CHANNELS, DH).astype(jnp.float32)
    grads = stream_grad.reshape(TEXT_POSITIONS, ASKING_CHANNELS, DH).astype(jnp.float32)
    cumulative = jnp.cumsum(linear_decay.astype(jnp.float32), axis=0)
    positions = jnp.arange(TEXT_POSITIONS, dtype=jnp.int32)

    def one_block(carry, block_index):
        key_accumulator, value_accumulator = carry
        begin = (block_index * block_rows).astype(jnp.int32)
        query_tile_block = lax.dynamic_slice_in_dim(query, begin, block_rows, 0)
        gradient_block = lax.dynamic_slice_in_dim(grads, begin, block_rows, 0)
        cum_block = lax.dynamic_slice_in_dim(cumulative, begin, block_rows, 0)
        pos_block = lax.dynamic_slice_in_dim(positions, begin, block_rows, 0)
        doc_block = lax.dynamic_slice_in_dim(document_ids, begin, block_rows, 0)
        log_ratio = cum_block.T[:, :, None] - cumulative.T[:, None, :]
        allowed = (positions[None, :] <= pos_block[:, None]) & (document_ids[None, :] == doc_block[:, None])
        decay_mask = jnp.where(allowed[None], jnp.exp(jnp.minimum(log_ratio, 0.0)), 0.0)
        dmix = decay_mask * jnp.einsum("tav,sav->ats", gradient_block, value_matrix, precision=highest)
        query_gradient = jnp.einsum("ats,sak->tak", dmix, key_matrix, precision=highest)
        key_accumulator = key_accumulator + jnp.einsum("ats,taq->saq", dmix, query_tile_block, precision=highest)
        mix = decay_mask * jnp.einsum("taq,saq->ats", query_tile_block, key_matrix, precision=highest)
        value_accumulator = value_accumulator + jnp.einsum("ats,tao->sao", mix, gradient_block, precision=highest)
        return (key_accumulator, value_accumulator), query_gradient.astype(jnp.bfloat16)

    zeros = jnp.zeros((TEXT_POSITIONS, ASKING_CHANNELS, DH), jnp.float32)
    (key_accumulator, value_accumulator), query_blocks = lax.scan(one_block, (zeros, zeros), jnp.arange(TEXT_POSITIONS // block_rows, dtype=jnp.int32))
    query_cotangent = query_blocks.reshape(TEXT_POSITIONS, ASKING_CHANNELS * DH)
    key_cotangent = key_accumulator.reshape(TEXT_POSITIONS, ASKING_CHANNELS * DH).astype(jnp.bfloat16)
    value_cotangent = value_accumulator.reshape(TEXT_POSITIONS, ASKING_CHANNELS * DH).astype(jnp.bfloat16)
    return query_cotangent, key_cotangent, value_cotangent


def reference(softmax_query, softmax_key, softmax_value, softmax_output, upstream_grad, linear_query, linear_key, linear_value, linear_decay, document_ids):
    key_gradient, value_gradient, stream_grad = softmax_part(softmax_query, softmax_key, softmax_value, softmax_output, upstream_grad, document_ids)
    query_cotangent, key_cotangent, value_cotangent = lightning_part(stream_grad, linear_query, linear_key, linear_value, linear_decay, document_ids)
    return (key_gradient, value_gradient, query_cotangent, key_cotangent, value_cotangent)
```

```python
import functools

import jax
import jax.numpy as jnp
from jax import lax
from jax.experimental import pallas as pl
from jax.experimental.pallas import tpu as pltpu
from jax.sharding import Mesh
from jax.sharding import PartitionSpec as P

very_low = -1e30
f32, bf16, i32 = jnp.float32, jnp.bfloat16, jnp.int32
DEC_ROWS = 16
VMEM = pl.BlockSpec(memory_space=pltpu.VMEM)
SMEM = pl.BlockSpec(memory_space=pltpu.SMEM)


def nt(a, b):
    return lax.dot_general(a, b, (((1,), (1,)), ((), ())), preferred_element_type=f32)


def nn(a, b):
    return lax.dot_general(a, b, (((1,), (0,)), ((), ())), preferred_element_type=f32)


def tn(a, b):
    return lax.dot_general(a, b, (((0,), (0,)), ((), ())), preferred_element_type=f32)


def iota(shape, dim):
    return lax.broadcasted_iota(i32, shape, dim)


def quot(x, d):
    return ((x.astype(f32) + 0.5) * (1.0 / d)).astype(i32)


def run_starts(docs):
    counts = []
    for v in (1, 2, 3):
        hit = jnp.where(docs < v, 1.0, 0.0)
        total = jnp.sum(jnp.sum(hit, axis=0, keepdims=True), axis=1, keepdims=True)
        counts.append(total.astype(i32))
    return counts


def start_of(pos, bounds):
    start = jnp.zeros_like(pos)
    for b in bounds:
        start = jnp.maximum(start, jnp.where(pos >= b, b, 0))
    return start


def chunks(count, body):
    if count <= 8:
        for i in range(count):
            body(i)
    else:
        lax.fori_loop(0, count, lambda i, c: (body(i), c)[1], 0)


def at(i, size):
    return pl.ds(i * size if isinstance(i, int) else pl.multiple_of(i * size, size), size)


def sums(dec_row):
    span = dec_row.shape[1]
    col, row = iota((span, span), 0), iota((span, span), 1)
    c_col = jnp.sum(jnp.where(row <= col, dec_row, 0.0), axis=1, keepdims=True)
    c_row = jnp.sum(jnp.where(row == col, c_col, 0.0), axis=0, keepdims=True)
    return c_row, c_col


def pack_linear(heads, idx_ref, q_ref, k_ref, v_ref, dec_ref, *rest):
    outs, scr = rest[:heads], rest[heads]
    tok, head = q_ref.shape[0], q_ref.shape[1] // heads
    p = lax.rem(idx_ref[0], heads)
    scr[...] = jnp.concatenate([dec_ref[...], jnp.zeros((tok, head - heads), f32)], axis=1).T
    for k in range(heads):
        h = p ^ k
        lanes = pl.ds(pl.multiple_of(h * head, head), head)
        out = outs[k]
        out[0:tok, :] = q_ref[:, lanes]
        out[tok : 2 * tok, :] = k_ref[:, lanes]
        out[2 * tok : 3 * tok, :] = v_ref[:, lanes]
        d = scr[pl.ds(h, 1), :]
        hi = d.astype(bf16)
        left = d - hi.astype(f32)
        mid = left.astype(bf16)
        low = (left - mid.astype(f32)).astype(bf16)
        r = iota((DEC_ROWS, head), 0)
        rows = jnp.where(r == 0, hi.astype(f32), jnp.where(r == 1, mid.astype(f32), jnp.where(r == 2, low.astype(f32), 0.0)))
        out[3 * tok : 3 * tok + DEC_ROWS, :] = rows.astype(bf16)


def pack_main(heads, planes, window, idx_ref, q_ref, k_ref, v_ref, o_ref, g_ref, out):
    tok, head = k_ref.shape
    rp, xs = tok // planes, heads // 2
    zx = lax.div(idx_ref[0], 2)
    wide = xs * planes * rp
    cols = []
    for a in range(heads):
        s = slice(a * head, (a + 1) * head)
        cols.append(jnp.sum(g_ref[:, s].astype(f32) * o_ref[:, s].astype(f32), axis=1, keepdims=True))
    r, lane = iota((tok, wide), 0), iota((tok, wide), 1) - zx * rp
    r8 = iota((8, wide), 0)
    for g in range(planes):
        hit = (lane == r - g * rp) & (lane >= 0) & (lane < rp)
        rows = [jnp.sum(jnp.where(hit, c, 0.0), axis=0, keepdims=True) for c in cols]
        for x in range(xs):
            to = g * xs + x
            s = slice(x * 2 * head, (x + 1) * 2 * head)
            out[to, 0:rp, :] = q_ref[g * rp : (g + 1) * rp, s]
            out[to, rp : 2 * rp, :] = g_ref[g * rp : (g + 1) * rp, s]
            for w in range(window):
                plane = (g - window + 1 + w) % planes
                rows_w = slice((2 + w) * rp, (3 + w) * rp)
                out[to, rows_w, 0:head] = k_ref[plane * rp : (plane + 1) * rp, :]
                out[to, rows_w, head : 2 * head] = v_ref[plane * rp : (plane + 1) * rp, :]
            d0, d1 = rows[2 * x], rows[2 * x + 1]
            h0, h1 = d0.astype(bf16).astype(f32), d1.astype(bf16).astype(f32)
            tail = jnp.where(r8 == 0, h0, jnp.where(r8 == 1, d0 - h0, jnp.where(r8 == 2, h1, jnp.where(r8 == 3, d1 - h1, 0.0))))
            out[to, (2 + window) * rp : (2 + window) * rp + 8, :] = tail.astype(bf16)


def pack_main_plain(heads, planes, window, idx, q, k, v, o, grad):
    tok, head = k.shape
    rp, xs = tok // planes, heads // 2
    zx = idx[0] // 2
    wide = xs * planes * rp

    def pieces(a):
        return a.reshape(planes, rp, xs, 2 * head).swapaxes(1, 2).reshape(planes * xs, rp, 2 * head)

    kv = jnp.concatenate([k, v], axis=1).reshape(planes, rp, 2 * head)
    win = jnp.stack([jnp.roll(kv, window - 1 - w, axis=0) for w in range(window)], axis=1)
    win = jnp.repeat(win.reshape(planes, 1, window * rp, 2 * head), xs, axis=1)
    win = win.reshape(planes * xs, window * rp, 2 * head)
    delta = jnp.sum((grad.astype(f32) * o.astype(f32)).reshape(tok, heads, head), axis=-1)
    high = lax.reduce_precision(delta, 8, 7)
    parts = jnp.stack([high, delta - high], axis=-1).astype(bf16)
    parts = parts.reshape(planes, rp, xs, 4).transpose(0, 2, 3, 1).reshape(planes * xs, 4, rp)
    tail = jnp.zeros((planes * xs, 8, wide), bf16)
    tail = lax.dynamic_update_slice(tail, parts, (0, 0, zx * rp))
    return jnp.concatenate([pieces(q), pieces(grad), win, tail], axis=1)


def gather_linear(heads, idx_ref, docs_ref, *rest):
    msgs, (qkv, dec, state) = rest[:heads], rest[heads:]
    tok, head = (msgs[0].shape[0] - DEC_ROWS) // 3, msgs[0].shape[1]
    p, g = lax.rem(idx_ref[0], heads), lax.div(idx_ref[0], heads)
    span = heads * tok
    for k in range(heads):
        off = pl.multiple_of((p ^ k) * tok, tok)
        for j in range(3):
            qkv[j, pl.ds(off, tok), :] = msgs[k][j * tok : (j + 1) * tok, :]
        parts = msgs[k][3 * tok : 3 * tok + DEC_ROWS, :].astype(f32)
        dec[:, pl.ds(off, tok)] = jnp.broadcast_to(jnp.sum(parts, axis=0, keepdims=True), (8, tok))
    bounds = run_starts(docs_ref[...])
    dec_row = dec[0:1, :]
    _, c_col = sums(dec_row)
    total = jnp.sum(dec_row, axis=1, keepdims=True)
    pos = g * span + iota((span, 1), 0)
    last = start_of(jnp.zeros((1, 1), i32) + (g * span + span - 1), bounds)
    tail = jnp.where(pos >= last, jnp.exp(jnp.minimum(total - c_col, 0.0)), 0.0)
    weighted = (qkv[2].astype(f32) * tail).astype(bf16)
    state[0:head, :] = tn(weighted, qkv[1])
    state[head : head + 8, :] = jnp.broadcast_to(total, (8, head))


def softmax_kernel(cfg, *refs):
    heads, planes, window, tok, aligned = cfg
    if aligned:
        idx_ref, docs_ref, own, other, qkv, dec, keep, give, stream_out, state, s_scr, p_scr, ds_scr = refs
    else:
        idx_ref, docs_ref, q_in, g_in, kv_in, delta_in, qkv, dec, keep, give, stream_out, state, s_scr, p_scr, ds_scr = refs
    head = keep.shape[1] // 2
    rp, owners = tok // planes, heads * planes // 2
    n = 2 * owners
    half_keys = owners * window * rp
    keys, span = 2 * half_keys, heads * tok
    scale = head ** (-0.5)
    me = idx_ref[0]
    core, g = lax.rem(me, 2), lax.div(me, heads)
    bounds = run_starts(docs_ref[...])

    if aligned:
        mine = pl.ds(pl.multiple_of(core * head, head), head)
        kv_rows = slice(2 * rp, (2 + window) * rp)

        def both(rows, lanes):
            count = owners * (rows.stop - rows.start)
            return jnp.concatenate([ref[:, rows, lanes].reshape(count, head) for ref in (own, other)], axis=0)

        q = both(slice(0, rp), mine)
        grad = both(slice(rp, 2 * rp), mine)
        key = both(kv_rows, slice(0, head))
        value = both(kv_rows, slice(head, 2 * head))
        tails = []
        for ref in (own, other):
            t = jnp.zeros((8, owners * rp), f32)
            for o in range(owners):
                t = t + ref[o, (2 + window) * rp : (2 + window) * rp + 8, :].astype(f32)
            tails.append(jnp.where(core == 0, t[0:1] + t[1:2], t[2:3] + t[3:4]))
        delta = jnp.concatenate(tails, axis=1)
    else:
        q, grad = q_in[...], g_in[...]
        key, value = kv_in[:, 0:head], kv_in[:, head : 2 * head]
        delta = delta_in[0:1, :]

    j = iota((1, span), 1)
    side = quot(j, owners * rp)
    inner = j - side * (owners * rp)
    zx = quot(inner, rp)
    q_rel = (inner - zx * rp) * n + zx * 2 + jnp.where(side == 0, core, 1 - core)
    q_pos = q_rel + g * span
    q_start = start_of(q_pos, bounds)

    def key_pos(first, count):
        j = iota((count, 1), 0) + first
        side = jnp.where(j >= half_keys, 1, 0)
        inner = j - side * half_keys
        zx = quot(inner, window * rp)
        row = inner - zx * (window * rp) + (g - window + 1) * rp
        row = jnp.where(row < 0, row + tok, row)
        return row * n + zx * 2 + jnp.where(side == 0, core, 1 - core)

    if aligned:
        wide, deep = 256, 256
    else:
        wide, deep = 128, 256
    steps = keys // deep
    for b in range(span // wide):
        lanes = slice(b * wide, (b + 1) * wide)
        qb, gb = q[lanes, :], grad[lanes, :]
        lo, hi, db = q_start[:, lanes], q_pos[:, lanes], delta[:, lanes]

        def first(i, best):
            rows = at(i, deep)
            kc = key[i * deep : (i + 1) * deep] if aligned else kv_in[rows, 0:head]
            s = nt(kc, qb)
            pos = key_pos(i * deep, deep)
            s = jnp.where((pos >= lo) & (pos <= hi), s, very_low)
            s_scr[rows, :] = s
            return jnp.maximum(best, jnp.max(s.reshape(deep // 8, 8, wide), axis=0))

        def second(i, acc):
            rows = at(i, deep)
            e = jnp.exp((s_scr[rows, :] - best) * scale)
            s_scr[rows, :] = e
            return acc + jnp.sum(e.reshape(deep // 8, 8, wide), axis=0)

        def third(i):
            rows = at(i, deep)
            vc = value[i * deep : (i + 1) * deep] if aligned else kv_in[rows, head : 2 * head]
            pr = s_scr[rows, :] * inv
            dp = nt(vc, gb)
            p_scr[rows, lanes] = pr.astype(bf16)
            ds_scr[rows, lanes] = (pr * (dp - db) * scale).astype(bf16)

        best = jnp.full((8, wide), very_low, f32)
        acc = jnp.zeros((8, wide), f32)
        if aligned:
            for i in range(steps):
                best = first(i, best)
            best = jnp.max(best, axis=0, keepdims=True)
            for i in range(steps):
                acc = second(i, acc)
            inv = 1.0 / jnp.sum(acc, axis=0, keepdims=True)
            for i in range(steps):
                third(i)
        else:
            best = jnp.max(lax.fori_loop(0, steps, first, best), axis=0, keepdims=True)
            inv = 1.0 / jnp.sum(lax.fori_loop(0, steps, second, acc), axis=0, keepdims=True)
            lax.fori_loop(0, steps, lambda i, c: (third(i), c)[1], 0)

    eye = jnp.where(iota((head, head), 0) == iota((head, head), 1), 1.0, 0.0).astype(bf16)
    dq_t = tn(key, ds_scr[...])
    stream_t = (nt(eye, grad) + dq_t).astype(bf16)
    order = jnp.where(iota((span, span), 0) == q_rel, 1.0, 0.0).astype(bf16)
    stream = nt(order, stream_t).astype(bf16)
    stream_out[...] = stream

    _, c_col = sums(dec[0:1, :])
    start = start_of(iota((span, 1), 0) + g * span, bounds)
    weight = jnp.where(start < g * span, jnp.exp(c_col), 0.0)
    state[0:head, :] = tn((stream.astype(f32) * weight).astype(bf16), qkv[0])
    state[head : head + 8, :] = jnp.broadcast_to(jnp.sum(dec[0:1, :], axis=1, keepdims=True), (8, head))

    for i, out in enumerate((keep, give)):
        rows = slice(i * half_keys, (i + 1) * half_keys)
        out[:, 0:head] = nn(ds_scr[rows, :], q).astype(out.dtype)
        out[:, head : 2 * head] = nn(p_scr[rows, :], grad).astype(out.dtype)


def joined(states, g, span, bounds, step):
    head = states[0].shape[1]
    one = jnp.zeros((1, 1), i32)
    total, passed = None, jnp.zeros((1, 1), f32)
    for k, ref in enumerate(states, 1):
        if step < 0:
            open_ = start_of(one + (g * span - 1), bounds) < (g - k + 1) * span
        else:
            open_ = start_of(one + ((g + k) * span - 1), bounds) < (g + 1) * span
        part = ref[0:head, :] * jnp.where(open_, jnp.exp(passed), 0.0)
        total = part if total is None else total + part
        passed = passed + ref[head : head + 1, 0:1]
    return total


def linear_kernel(heads, idx_ref, docs_ref, stream_ref, qkv, dec, *rest):
    states, (q_out, k_out, v_out, dm, mx) = rest[:-5], rest[-5:]
    span, head = stream_ref.shape
    g = lax.div(idx_ref[0], heads)
    bounds = run_starts(docs_ref[...])
    earlier = joined(states, g, span, bounds, -1)
    c_row, c_col = sums(dec[0:1, :])
    stream, query, key, value = stream_ref[...], qkv[0], qkv[1], qkv[2]
    t = iota((1, span), 1)
    lo = start_of(t + g * span, bounds) - g * span
    deep = 128
    for i in range(span // deep):
        rows = slice(i * deep, (i + 1) * deep)
        s = iota((deep, 1), 0) + i * deep
        ratio = jnp.minimum(c_row - c_col[rows], 0.0)
        decay = jnp.where((s <= t) & (s >= lo), jnp.exp(ratio), 0.0)
        dm[rows, :] = (decay * nt(value[rows], stream)).astype(bf16)
        mx[rows, :] = (decay * nt(key[rows], query)).astype(bf16)
    start = start_of(iota((span, 1), 0) + g * span, bounds)
    weight = jnp.where(start < g * span, jnp.exp(c_col), 0.0)
    q_out[...] = (tn(dm[...], key) + weight * nn(stream, earlier.astype(bf16))).astype(bf16)
    k_out[...] = nn(dm[...], query)
    v_out[...] = nn(mx[...], stream)


def finish_kernel(heads, idx_ref, docs_ref, q_ref, k_ref, v_ref, qkv, dec, *rest):
    states, outs, (k_scr, v_scr) = rest[: -2 - heads], rest[-2 - heads : -2], rest[-2:]
    span, head = q_ref.shape
    tok = span // heads
    p, g = lax.rem(idx_ref[0], heads), lax.div(idx_ref[0], heads)
    bounds = run_starts(docs_ref[...])
    later = joined(states, g, span, bounds, 1).astype(bf16)
    _, c_col = sums(dec[0:1, :])
    total = jnp.sum(dec[0:1, :], axis=1, keepdims=True)
    pos = g * span + iota((span, 1), 0)
    last = start_of(jnp.zeros((1, 1), i32) + (g * span + span - 1), bounds)
    tail = jnp.where(pos >= last, jnp.exp(jnp.minimum(total - c_col, 0.0)), 0.0)
    k_scr[...] = (k_ref[...] + tail * nn(qkv[2], later)).astype(bf16)
    v_scr[...] = (v_ref[...] + tail * nt(qkv[1], later)).astype(bf16)
    for k in range(heads):
        rows = pl.ds(pl.multiple_of((p ^ k) * tok, tok), tok)
        outs[k][0:tok, :] = q_ref[rows, :]
        outs[k][tok : 2 * tok, :] = k_scr[rows, :]
        outs[k][2 * tok : 3 * tok, :] = v_scr[rows, :]


def spread_kernel(heads, idx_ref, *rest):
    msgs, outs = rest[:heads], rest[heads:]
    tok, head = outs[0].shape[0], outs[0].shape[1] // heads
    p = lax.rem(idx_ref[0], heads)
    for k in range(heads):
        lanes = pl.ds(pl.multiple_of((p ^ k) * head, head), head)
        for j in range(3):
            outs[j][:, lanes] = msgs[k][j * tok : (j + 1) * tok, :]


def total_kernel(planes, xs, window, parts, k_out, v_out):
    tok, head = k_out.shape
    rp = tok // planes
    for q in range(planes):
        total = None
        for j in range(window):
            w = window - 1 - j
            for x in range(xs):
                part = parts[((q + j) % planes) * xs + x, w * rp : (w + 1) * rp, :].astype(f32)
                total = part if total is None else total + part
        rows = slice(q * rp, (q + 1) * rp)
        k_out[rows, :] = total[:, 0:head].astype(bf16)
        v_out[rows, :] = total[:, head : 2 * head].astype(bf16)


def call(body, ins, outs, scratch=(), flops=1 << 20):
    in_specs = [SMEM if a.dtype == i32 and a.ndim == 1 else VMEM for a in ins]
    return pl.pallas_call(
        body,
        in_specs=in_specs,
        out_specs=tuple(VMEM for _ in outs),
        out_shape=tuple(jax.ShapeDtypeStruct(*o) for o in outs),
        scratch_shapes=list(scratch),
        compiler_params=pltpu.CompilerParams(vmem_limit_bytes=60000 * 1024),
        cost_estimate=pl.CostEstimate(flops=flops, bytes_accessed=1 << 20, transcendentals=0),
    )(*ins)


def body(
    softmax_query,
    softmax_key,
    softmax_value,
    softmax_output,
    upstream_grad,
    linear_query,
    linear_key,
    linear_value,
    linear_decay,
    document_ids,
):
    tok, head = softmax_key.shape
    heads = softmax_query.shape[1] // head
    n = lax.axis_size("zx") * lax.axis_size("core")
    planes, xs = n // heads, heads // 2
    rp = tok // planes
    window = min(planes, planes // 2 + 1)
    owners = n // 2
    span = heads * tok
    half_keys = owners * window * rp
    aligned = rp % 16 == 0
    me = (lax.axis_index("zx") * 2 + lax.axis_index("core")).astype(i32)
    idx = me.reshape(1)
    docs = document_ids.reshape(-1, 128)
    line = ("zx", "core")

    def swap(a, k):
        return lax.ppermute(a, line, [(i, i ^ k) for i in range(n)])

    def shift(a, k):
        pairs = [(i, i + k * heads) for i in range(n) if 0 <= i + k * heads < n]
        return lax.ppermute(a, line, pairs)

    msg = ((3 * tok + DEC_ROWS, head), bf16)
    lin = call(
        functools.partial(pack_linear, heads),
        (idx, linear_query, linear_key, linear_value, linear_decay),
        (msg,) * heads,
        [pltpu.VMEM((head, tok), f32)],
    )
    lin = [lin[0]] + [swap(lin[k], k) for k in range(1, heads)]

    packed = (idx, softmax_query, softmax_key, softmax_value, softmax_output, upstream_grad)
    if aligned:
        rows = (2 + window) * rp + 8
        send = call(
            functools.partial(pack_main, heads, planes, window), packed, (((owners, rows, 2 * head), bf16),)
        )[0]
    else:
        send = pack_main_plain(heads, planes, window, *packed)
    own = lax.all_to_all(send, "zx", 0, 0, tiled=True)
    other = swap(own, 1)

    state = ((head + 8, head), f32)
    qkv, dec, forward = call(
        functools.partial(gather_linear, heads),
        (idx, docs, *lin),
        (((3, span, head), bf16), ((8, span), f32), state),
    )
    before = [shift(forward, k) for k in range(1, window)]

    if aligned:
        given = (own, other)
        wide = 256
    else:
        core = me % 2
        halves = [lax.dynamic_slice_in_dim(a, core * head, head, 2) for a in (own, other)]
        q = jnp.concatenate([a[:, 0:rp].reshape(owners * rp, head) for a in halves])
        grad = jnp.concatenate([a[:, rp : 2 * rp].reshape(owners * rp, head) for a in halves])
        kv = jnp.concatenate([a[:, 2 * rp : -8].reshape(half_keys, 2 * head) for a in (own, other)])
        tails = [jnp.sum(a[:, -8:].astype(f32), axis=0) for a in (own, other)]
        tails = jnp.concatenate(tails, axis=1)
        delta = jnp.where(core == 0, tails[0] + tails[1], tails[2] + tails[3])
        given = (q, grad, kv, jnp.broadcast_to(delta[None], (8, span)))
        wide = 128
    keep, give, stream, backward = call(
        functools.partial(softmax_kernel, (heads, planes, window, tok, aligned)),
        (idx, docs, *given, qkv, dec),
        (((half_keys, 2 * head), f32), ((half_keys, 2 * head), bf16), ((span, head), bf16), state),
        [
            pltpu.VMEM((2 * half_keys, wide), f32),
            pltpu.VMEM((2 * half_keys, span), bf16),
            pltpu.VMEM((2 * half_keys, span), bf16),
        ],
        flops=1 << 30,
    )
    after = [shift(backward, -k) for k in range(1, window)]
    taken = swap(give, 1)
    parts = (keep + taken.astype(f32)).astype(bf16).reshape(owners, window * rp, 2 * head)
    parts = lax.all_to_all(parts, "zx", 0, 0, tiled=True)

    square = [pltpu.VMEM((span, span), bf16)] * 2
    q_cot, k_part, v_part = call(
        functools.partial(linear_kernel, heads),
        (idx, docs, stream, qkv, dec, *before),
        (((span, head), bf16), ((span, head), f32), ((span, head), f32)),
        square,
        flops=1 << 28,
    )
    out = ((3 * tok, head), bf16)
    msgs = call(
        functools.partial(finish_kernel, heads),
        (idx, docs, q_cot, k_part, v_part, qkv, dec, *after),
        (out,) * heads,
        [pltpu.VMEM((span, head), bf16)] * 2,
    )
    msgs = [msgs[0]] + [swap(msgs[k], k) for k in range(1, heads)]
    whole = ((tok, heads * head), bf16)
    q_out, k_out, v_out = call(functools.partial(spread_kernel, heads), (idx, *msgs), (whole,) * 3)

    if aligned:
        one = ((tok, head), bf16)
        key_rows, value_rows = call(
            functools.partial(total_kernel, planes, xs, window), (parts,), (one, one)
        )
    else:
        split = parts.reshape(planes, xs, window, rp, 2 * head).astype(f32).sum(axis=1)
        total = sum(jnp.roll(split[:, window - 1 - j], -j, axis=0) for j in range(window))
        total = total.reshape(tok, 2 * head).astype(bf16)
        key_rows, value_rows = total[:, 0:head], total[:, head:]
    return key_rows, value_rows, q_out, k_out, v_out


def solution(mesh):
    groups, ctx = mesh.devices.shape
    fine = Mesh(mesh.devices.reshape(groups, ctx // 2, 2), ("groups", "zx", "core"))
    rows = P(("groups", "zx", "core"), None)
    return jax.shard_map(
        body,
        mesh=fine,
        in_specs=(rows,) * 9 + (P("groups"),),
        out_specs=(rows,) * 5,
        check_vma=False,
    )
```

```python
import functools

import jax
import jax.numpy as jnp
from jax import lax
from jax.experimental import pallas as pl
from jax.experimental.pallas import tpu as pltpu
from jax.sharding import Mesh
from jax.sharding import PartitionSpec as P

very_low = -1e30
f32, bf16, i32 = jnp.float32, jnp.bfloat16, jnp.int32
DEC_ROWS = 16
VMEM = pl.BlockSpec(memory_space=pltpu.VMEM)
SMEM = pl.BlockSpec(memory_space=pltpu.SMEM)
HBM = pl.BlockSpec(memory_space=pltpu.HBM)


def nt(a, b):
    return lax.dot_general(a, b, (((1,), (1,)), ((), ())), preferred_element_type=f32)


def nn(a, b):
    return lax.dot_general(a, b, (((1,), (0,)), ((), ())), preferred_element_type=f32)


def tn(a, b):
    return lax.dot_general(a, b, (((0,), (0,)), ((), ())), preferred_element_type=f32)


def iota(shape, dim):
    return lax.broadcasted_iota(i32, shape, dim)


def quot(x, d):
    return ((x.astype(f32) + 0.5) * (1.0 / d)).astype(i32)


def run_starts(docs):
    counts = []
    for v in (1, 2, 3):
        hit = jnp.where(docs < v, 1.0, 0.0)
        total = jnp.sum(jnp.sum(hit, axis=0, keepdims=True), axis=1, keepdims=True)
        counts.append(total.astype(i32))
    return counts


def start_of(pos, bounds):
    start = jnp.zeros_like(pos)
    for b in bounds:
        start = jnp.maximum(start, jnp.where(pos >= b, b, 0))
    return start


def chunks(count, body):
    if count <= 8:
        for i in range(count):
            body(i)
    else:
        lax.fori_loop(0, count, lambda i, c: (body(i), c)[1], 0)


def at(i, size):
    return pl.ds(i * size if isinstance(i, int) else pl.multiple_of(i * size, size), size)


def sums(dec_row):
    span = dec_row.shape[1]
    col, row = iota((span, span), 0), iota((span, span), 1)
    c_col = jnp.sum(jnp.where(row <= col, dec_row, 0.0), axis=1, keepdims=True)
    c_row = jnp.sum(jnp.where(row == col, c_col, 0.0), axis=0, keepdims=True)
    return c_row, c_col


def pack_linear(heads, idx_ref, q_ref, k_ref, v_ref, dec_ref, outs):
    tok, head = q_ref.shape[0], q_ref.shape[1] // heads
    p = lax.rem(idx_ref[0], heads)
    for k in range(heads):
        h = p ^ k
        lanes = pl.ds(pl.multiple_of(h * head, head), head)
        out = outs[k]
        out[0:tok, :] = q_ref[:, lanes]
        out[tok : 2 * tok, :] = k_ref[:, lanes]
        out[2 * tok : 3 * tok, :] = v_ref[:, lanes]
        d = dec_ref[pl.ds(h, 1), :]
        hi = d.astype(bf16).astype(f32)
        mid = (d - hi).astype(bf16).astype(f32)
        low = d - hi - mid
        r = iota((DEC_ROWS, tok), 0)
        rows = jnp.where(r == 0, hi, jnp.where(r == 1, mid, jnp.where(r == 2, low, 0.0)))
        out[3 * tok : 3 * tok + DEC_ROWS, :] = rows.astype(bf16)


def pack_main(heads, planes, window, idx_ref, q_ref, k_ref, v_ref, o_ref, g_ref, out):
    tok, head = k_ref.shape
    rp, xs = tok // planes, heads // 2
    zx = lax.div(idx_ref[0], 2)
    wide = xs * planes * rp
    cols = []
    for a in range(heads):
        s = slice(a * head, (a + 1) * head)
        cols.append(jnp.sum(g_ref[:, s].astype(f32) * o_ref[:, s].astype(f32), axis=1, keepdims=True))
    r, lane = iota((tok, wide), 0), iota((tok, wide), 1) - zx * rp
    r8 = iota((8, wide), 0)
    for g in range(planes):
        hit = (lane == r - g * rp) & (lane >= 0) & (lane < rp)
        rows = [jnp.sum(jnp.where(hit, c, 0.0), axis=0, keepdims=True) for c in cols]
        for x in range(xs):
            to = g * xs + x
            s = slice(x * 2 * head, (x + 1) * 2 * head)
            out[to, 0:rp, :] = q_ref[g * rp : (g + 1) * rp, s]
            out[to, rp : 2 * rp, :] = g_ref[g * rp : (g + 1) * rp, s]
            for w in range(window):
                plane = (g - window + 1 + w) % planes
                rows_w = slice((2 + w) * rp, (3 + w) * rp)
                out[to, rows_w, 0:head] = k_ref[plane * rp : (plane + 1) * rp, :]
                out[to, rows_w, head : 2 * head] = v_ref[plane * rp : (plane + 1) * rp, :]
            d0, d1 = rows[2 * x], rows[2 * x + 1]
            h0, h1 = d0.astype(bf16).astype(f32), d1.astype(bf16).astype(f32)
            tail = jnp.where(r8 == 0, h0, jnp.where(r8 == 1, d0 - h0, jnp.where(r8 == 2, h1, jnp.where(r8 == 3, d1 - h1, 0.0))))
            out[to, (2 + window) * rp : (2 + window) * rp + 8, :] = tail.astype(bf16)


def pack_kernel(heads, planes, window, count, idx_ref, *refs):
    ins, outs, held, sem = refs[:count], refs[count : -count - 1], refs[-count - 1 : -1], refs[-1]
    copies = [pltpu.make_async_copy(a, b, sem.at[i]) for i, (a, b) in enumerate(zip(ins, held))]
    for c in copies:
        c.start()
    for c in copies[-4:]:
        c.wait()
    pack_linear(heads, idx_ref, *held[-4:], outs[-heads:])
    if window:
        for c in copies[:-4]:
            c.wait()
        pack_main(heads, planes, window, idx_ref, *held[:5], outs[0])


def pack_main_plain(heads, planes, window, idx, q, k, v, o, grad):
    tok, head = k.shape
    rp, xs = tok // planes, heads // 2
    zx = idx[0] // 2
    wide = xs * planes * rp

    def pieces(a):
        return a.reshape(planes, rp, xs, 2 * head).swapaxes(1, 2).reshape(planes * xs, rp, 2 * head)

    kv = jnp.concatenate([k, v], axis=1).reshape(planes, rp, 2 * head)
    win = jnp.stack([jnp.roll(kv, window - 1 - w, axis=0) for w in range(window)], axis=1)
    win = jnp.repeat(win.reshape(planes, 1, window * rp, 2 * head), xs, axis=1)
    win = win.reshape(planes * xs, window * rp, 2 * head)
    delta = jnp.sum((grad.astype(f32) * o.astype(f32)).reshape(tok, heads, head), axis=-1)
    high = lax.reduce_precision(delta, 8, 7)
    parts = jnp.stack([high, delta - high], axis=-1).astype(bf16)
    parts = parts.reshape(planes, rp, xs, 4).transpose(0, 2, 3, 1).reshape(planes * xs, 4, rp)
    tail = jnp.zeros((planes * xs, 8, wide), bf16)
    tail = lax.dynamic_update_slice(tail, parts, (0, 0, zx * rp))
    return jnp.concatenate([pieces(q), pieces(grad), win, tail], axis=1)


def gather_linear(heads, idx_ref, docs_ref, *rest):
    msgs, (qkv, dec, state) = rest[:heads], rest[heads:]
    tok, head = (msgs[0].shape[0] - DEC_ROWS) // 3, msgs[0].shape[1]
    p, g = lax.rem(idx_ref[0], heads), lax.div(idx_ref[0], heads)
    span = heads * tok
    for k in range(heads):
        off = pl.multiple_of((p ^ k) * tok, tok)
        for j in range(3):
            qkv[j, pl.ds(off, tok), :] = msgs[k][j * tok : (j + 1) * tok, :]
        parts = msgs[k][3 * tok : 3 * tok + DEC_ROWS, :].astype(f32)
        dec[:, pl.ds(off, tok)] = jnp.broadcast_to(jnp.sum(parts, axis=0, keepdims=True), (8, tok))
    bounds = run_starts(docs_ref[...])
    dec_row = dec[0:1, :]
    _, c_col = sums(dec_row)
    total = jnp.sum(dec_row, axis=1, keepdims=True)
    pos = g * span + iota((span, 1), 0)
    last = start_of(jnp.zeros((1, 1), i32) + (g * span + span - 1), bounds)
    tail = jnp.where(pos >= last, jnp.exp(jnp.minimum(total - c_col, 0.0)), 0.0)
    weighted = (qkv[2].astype(f32) * tail).astype(bf16)
    state[0:head, :] = tn(weighted, qkv[1])
    state[head : head + 8, :] = jnp.broadcast_to(total, (8, head))


def softmax_kernel(cfg, *refs):
    heads, planes, window, tok, aligned = cfg
    if aligned:
        idx_ref, docs_ref, own, other, qkv, dec, keep, give, stream_out, state, s_scr, p_scr, ds_scr = refs
    else:
        idx_ref, docs_ref, q_in, g_in, kv_in, delta_in, qkv, dec, keep, give, stream_out, state, s_scr, p_scr, ds_scr = refs
    head = keep.shape[1] // 2
    rp, owners = tok // planes, heads * planes // 2
    n = 2 * owners
    half_keys = owners * window * rp
    keys, span = 2 * half_keys, heads * tok
    scale = head ** (-0.5)
    me = idx_ref[0]
    core, g = lax.rem(me, 2), lax.div(me, heads)
    bounds = run_starts(docs_ref[...])

    if aligned:
        mine = pl.ds(pl.multiple_of(core * head, head), head)
        kv_rows = slice(2 * rp, (2 + window) * rp)

        def both(rows, lanes):
            count = owners * (rows.stop - rows.start)
            return jnp.concatenate([ref[:, rows, lanes].reshape(count, head) for ref in (own, other)], axis=0)

        q = both(slice(0, rp), mine)
        grad = both(slice(rp, 2 * rp), mine)
        key = both(kv_rows, slice(0, head))
        value = both(kv_rows, slice(head, 2 * head))
        tails = []
        for ref in (own, other):
            t = jnp.zeros((8, owners * rp), f32)
            for o in range(owners):
                t = t + ref[o, (2 + window) * rp : (2 + window) * rp + 8, :].astype(f32)
            tails.append(jnp.where(core == 0, t[0:1] + t[1:2], t[2:3] + t[3:4]))
        delta = jnp.concatenate(tails, axis=1)
    else:
        q, grad = q_in[...], g_in[...]
        key, value = kv_in[:, 0:head], kv_in[:, head : 2 * head]
        delta = delta_in[0:1, :]

    j = iota((1, span), 1)
    side = quot(j, owners * rp)
    inner = j - side * (owners * rp)
    zx = quot(inner, rp)
    q_rel = (inner - zx * rp) * n + zx * 2 + jnp.where(side == 0, core, 1 - core)
    q_pos = q_rel + g * span
    q_start = start_of(q_pos, bounds)

    def key_pos(first, count):
        j = iota((count, 1), 0) + first
        side = jnp.where(j >= half_keys, 1, 0)
        inner = j - side * half_keys
        zx = quot(inner, window * rp)
        row = inner - zx * (window * rp) + (g - window + 1) * rp
        row = jnp.where(row < 0, row + tok, row)
        return row * n + zx * 2 + jnp.where(side == 0, core, 1 - core)

    if aligned:
        wide, deep = 256, 256
    else:
        wide, deep = 128, 256
    steps = keys // deep
    for b in range(span // wide):
        lanes = slice(b * wide, (b + 1) * wide)
        qb, gb = q[lanes, :], grad[lanes, :]
        lo, hi, db = q_start[:, lanes], q_pos[:, lanes], delta[:, lanes]

        def first(i, best):
            rows = at(i, deep)
            kc = key[i * deep : (i + 1) * deep] if aligned else kv_in[rows, 0:head]
            s = nt(kc, qb)
            pos = key_pos(i * deep, deep)
            s = jnp.where((pos >= lo) & (pos <= hi), s, very_low)
            s_scr[rows, :] = s
            return jnp.maximum(best, jnp.max(s.reshape(deep // 8, 8, wide), axis=0))

        def second(i, acc):
            rows = at(i, deep)
            e = jnp.exp((s_scr[rows, :] - best) * scale)
            s_scr[rows, :] = e
            return acc + jnp.sum(e.reshape(deep // 8, 8, wide), axis=0)

        def third(i):
            rows = at(i, deep)
            vc = value[i * deep : (i + 1) * deep] if aligned else kv_in[rows, head : 2 * head]
            pr = s_scr[rows, :] * inv
            dp = nt(vc, gb)
            p_scr[rows, lanes] = pr.astype(bf16)
            ds_scr[rows, lanes] = (pr * (dp - db) * scale).astype(bf16)

        best = jnp.full((8, wide), very_low, f32)
        acc = jnp.zeros((8, wide), f32)
        if aligned:
            for i in range(steps):
                best = first(i, best)
            best = jnp.max(best, axis=0, keepdims=True)
            for i in range(steps):
                acc = second(i, acc)
            inv = 1.0 / jnp.sum(acc, axis=0, keepdims=True)
            for i in range(steps):
                third(i)
        else:
            best = jnp.max(lax.fori_loop(0, steps, first, best), axis=0, keepdims=True)
            inv = 1.0 / jnp.sum(lax.fori_loop(0, steps, second, acc), axis=0, keepdims=True)
            lax.fori_loop(0, steps, lambda i, c: (third(i), c)[1], 0)

    eye = jnp.where(iota((head, head), 0) == iota((head, head), 1), 1.0, 0.0).astype(bf16)
    dq_t = tn(key, ds_scr[...])
    stream_t = (nt(eye, grad) + dq_t).astype(bf16)
    order = jnp.where(iota((span, span), 0) == q_rel, 1.0, 0.0).astype(bf16)
    stream = nt(order, stream_t).astype(bf16)
    stream_out[...] = stream

    _, c_col = sums(dec[0:1, :])
    start = start_of(iota((span, 1), 0) + g * span, bounds)
    weight = jnp.where(start < g * span, jnp.exp(c_col), 0.0)
    state[0:head, :] = tn((stream.astype(f32) * weight).astype(bf16), qkv[0])
    state[head : head + 8, :] = jnp.broadcast_to(jnp.sum(dec[0:1, :], axis=1, keepdims=True), (8, head))

    for i, out in enumerate((keep, give)):
        rows = slice(i * half_keys, (i + 1) * half_keys)
        out[:, 0:head] = nn(ds_scr[rows, :], q).astype(out.dtype)
        out[:, head : 2 * head] = nn(p_scr[rows, :], grad).astype(out.dtype)


def joined(states, g, span, bounds, step):
    head = states[0].shape[1]
    one = jnp.zeros((1, 1), i32)
    total, passed = None, jnp.zeros((1, 1), f32)
    for k, ref in enumerate(states, 1):
        if step < 0:
            open_ = start_of(one + (g * span - 1), bounds) < (g - k + 1) * span
        else:
            open_ = start_of(one + ((g + k) * span - 1), bounds) < (g + 1) * span
        part = ref[0:head, :] * jnp.where(open_, jnp.exp(passed), 0.0)
        total = part if total is None else total + part
        passed = passed + ref[head : head + 1, 0:1]
    return total


def linear_kernel(heads, idx_ref, docs_ref, stream_ref, qkv, dec, *rest):
    states, (q_out, k_out, v_out, dm, mx) = rest[:-5], rest[-5:]
    span, head = stream_ref.shape
    g = lax.div(idx_ref[0], heads)
    bounds = run_starts(docs_ref[...])
    earlier = joined(states, g, span, bounds, -1)
    c_row, c_col = sums(dec[0:1, :])
    stream, query, key, value = stream_ref[...], qkv[0], qkv[1], qkv[2]
    t = iota((1, span), 1)
    lo = start_of(t + g * span, bounds) - g * span
    deep = 128
    for i in range(span // deep):
        rows = slice(i * deep, (i + 1) * deep)
        s = iota((deep, 1), 0) + i * deep
        ratio = jnp.minimum(c_row - c_col[rows], 0.0)
        decay = jnp.where((s <= t) & (s >= lo), jnp.exp(ratio), 0.0)
        dm[rows, :] = (decay * nt(value[rows], stream)).astype(bf16)
        mx[rows, :] = (decay * nt(key[rows], query)).astype(bf16)
    start = start_of(iota((span, 1), 0) + g * span, bounds)
    weight = jnp.where(start < g * span, jnp.exp(c_col), 0.0)
    q_out[...] = (tn(dm[...], key) + weight * nn(stream, earlier.astype(bf16))).astype(bf16)
    k_out[...] = nn(dm[...], query)
    v_out[...] = nn(mx[...], stream)


def finish_kernel(heads, idx_ref, docs_ref, q_ref, k_ref, v_ref, qkv, dec, *rest):
    states, outs, (k_scr, v_scr) = rest[: -2 - heads], rest[-2 - heads : -2], rest[-2:]
    span, head = q_ref.shape
    tok = span // heads
    p, g = lax.rem(idx_ref[0], heads), lax.div(idx_ref[0], heads)
    bounds = run_starts(docs_ref[...])
    later = joined(states, g, span, bounds, 1).astype(bf16)
    _, c_col = sums(dec[0:1, :])
    total = jnp.sum(dec[0:1, :], axis=1, keepdims=True)
    pos = g * span + iota((span, 1), 0)
    last = start_of(jnp.zeros((1, 1), i32) + (g * span + span - 1), bounds)
    tail = jnp.where(pos >= last, jnp.exp(jnp.minimum(total - c_col, 0.0)), 0.0)
    k_scr[...] = (k_ref[...] + tail * nn(qkv[2], later)).astype(bf16)
    v_scr[...] = (v_ref[...] + tail * nt(qkv[1], later)).astype(bf16)
    for k in range(heads):
        rows = pl.ds(pl.multiple_of((p ^ k) * tok, tok), tok)
        outs[k][0:tok, :] = q_ref[rows, :]
        outs[k][tok : 2 * tok, :] = k_scr[rows, :]
        outs[k][2 * tok : 3 * tok, :] = v_scr[rows, :]


def spread_kernel(heads, idx_ref, *rest):
    msgs, outs = rest[:heads], rest[heads:]
    tok, head = outs[0].shape[0], outs[0].shape[1] // heads
    p = lax.rem(idx_ref[0], heads)
    for k in range(heads):
        lanes = pl.ds(pl.multiple_of((p ^ k) * head, head), head)
        for j in range(3):
            outs[j][:, lanes] = msgs[k][j * tok : (j + 1) * tok, :]


def total_kernel(planes, xs, window, parts, k_out, v_out):
    tok, head = k_out.shape
    rp = tok // planes
    for q in range(planes):
        total = None
        for j in range(window):
            w = window - 1 - j
            for x in range(xs):
                part = parts[((q + j) % planes) * xs + x, w * rp : (w + 1) * rp, :].astype(f32)
                total = part if total is None else total + part
        rows = slice(q * rp, (q + 1) * rp)
        k_out[rows, :] = total[:, 0:head].astype(bf16)
        v_out[rows, :] = total[:, head : 2 * head].astype(bf16)


def call(body, ins, outs, scratch=(), flops=1 << 20, grant=8, space=VMEM):
    in_specs = [SMEM if a.dtype == i32 and a.ndim == 1 else space for a in ins]
    return pl.pallas_call(
        body,
        in_specs=in_specs,
        out_specs=tuple(VMEM for _ in outs),
        out_shape=tuple(jax.ShapeDtypeStruct(*o) for o in outs),
        scratch_shapes=list(scratch),
        compiler_params=pltpu.CompilerParams(vmem_limit_bytes=grant << 20),
        cost_estimate=pl.CostEstimate(flops=flops, bytes_accessed=1 << 20, transcendentals=0),
    )(*ins)


def body(
    softmax_query,
    softmax_key,
    softmax_value,
    softmax_output,
    upstream_grad,
    linear_query,
    linear_key,
    linear_value,
    linear_decay,
    document_ids,
):
    tok, head = softmax_key.shape
    heads = softmax_query.shape[1] // head
    n = lax.axis_size("zx") * lax.axis_size("core")
    planes, xs = n // heads, heads // 2
    rp = tok // planes
    window = min(planes, planes // 2 + 1)
    owners = n // 2
    span = heads * tok
    half_keys = owners * window * rp
    aligned = rp % 16 == 0
    me = (lax.axis_index("zx") * 2 + lax.axis_index("core")).astype(i32)
    idx = me.reshape(1)
    docs = document_ids.reshape(-1, 128)
    line = ("zx", "core")

    def swap(a, k):
        return lax.ppermute(a, line, [(i, i ^ k) for i in range(n)])

    def shift(a, k):
        pairs = [(i, i + k * heads) for i in range(n) if 0 <= i + k * heads < n]
        return lax.ppermute(a, line, pairs)

    msg = ((3 * tok + DEC_ROWS, head), bf16)
    packed = (softmax_query, softmax_key, softmax_value, softmax_output, upstream_grad)
    linear = (linear_query, linear_key, linear_value, linear_decay.T)
    if aligned:
        rows = (2 + window) * rp + 8
        send, *lin = call(
            functools.partial(pack_kernel, heads, planes, window, 9),
            (idx, *packed, *linear),
            (((owners, rows, 2 * head), bf16),) + (msg,) * heads,
            [pltpu.VMEM(a.shape, a.dtype) for a in (*packed, *linear)] + [pltpu.SemaphoreType.DMA((9,))],
            space=HBM,
        )
    else:
        send = pack_main_plain(heads, planes, window, idx, *packed)
        lin = call(
            functools.partial(pack_kernel, heads, planes, 0, 4),
            (idx, *linear),
            (msg,) * heads,
            [pltpu.VMEM(a.shape, a.dtype) for a in linear] + [pltpu.SemaphoreType.DMA((4,))],
            space=HBM,
        )
    own = lax.all_to_all(send, "zx", 0, 0, tiled=True)
    lin = [lin[0]] + [swap(lin[k], k) for k in range(1, heads)]

    state = ((head + 8, head), f32)
    qkv, dec, forward = call(
        functools.partial(gather_linear, heads),
        (idx, docs, *lin),
        (((3, span, head), bf16), ((8, span), f32), state),
    )
    own, forward = lax.optimization_barrier((own, forward))
    before = [shift(forward, k) for k in range(1, window)]
    other = swap(own, 1)

    if aligned:
        given = (own, other)
        wide = 256
    else:
        core = me % 2
        halves = [lax.dynamic_slice_in_dim(a, core * head, head, 2) for a in (own, other)]
        q = jnp.concatenate([a[:, 0:rp].reshape(owners * rp, head) for a in halves])
        grad = jnp.concatenate([a[:, rp : 2 * rp].reshape(owners * rp, head) for a in halves])
        kv = jnp.concatenate([a[:, 2 * rp : -8].reshape(half_keys, 2 * head) for a in (own, other)])
        tails = [jnp.sum(a[:, -8:].astype(f32), axis=0) for a in (own, other)]
        tails = jnp.concatenate(tails, axis=1)
        delta = jnp.where(core == 0, tails[0] + tails[1], tails[2] + tails[3])
        given = (q, grad, kv, jnp.broadcast_to(delta[None], (8, span)))
        wide = 128
    keep, give, stream, backward = call(
        functools.partial(softmax_kernel, (heads, planes, window, tok, aligned)),
        (idx, docs, *given, qkv, dec),
        (((half_keys, 2 * head), f32), ((half_keys, 2 * head), bf16), ((span, head), bf16), state),
        [
            pltpu.VMEM((2 * half_keys, wide), f32),
            pltpu.VMEM((2 * half_keys, span), bf16),
            pltpu.VMEM((2 * half_keys, span), bf16),
        ],
        flops=1 << 30,
        grant=24 if aligned else 58,
    )
    taken = swap(give, 1)
    after = [shift(backward, -k) for k in range(1, window)]
    square = [pltpu.VMEM((span, span), bf16)] * 2
    q_cot, k_part, v_part = call(
        functools.partial(linear_kernel, heads),
        (idx, docs, stream, qkv, dec, *before),
        (((span, head), bf16), ((span, head), f32), ((span, head), f32)),
        square,
        flops=1 << 28,
        grant=16,
    )
    taken, k_part, *after = lax.optimization_barrier((taken, k_part, *after))
    parts = (keep + taken.astype(f32)).astype(bf16).reshape(owners, window * rp, 2 * head)
    parts = lax.all_to_all(parts, "zx", 0, 0, tiled=True)

    out = ((3 * tok, head), bf16)
    msgs = call(
        functools.partial(finish_kernel, heads),
        (idx, docs, q_cot, k_part, v_part, qkv, dec, *after),
        (out,) * heads,
        [pltpu.VMEM((span, head), bf16)] * 2,
    )
    msgs = [msgs[0]] + [swap(msgs[k], k) for k in range(1, heads)]
    whole = ((tok, heads * head), bf16)
    q_out, k_out, v_out = call(functools.partial(spread_kernel, heads), (idx, *msgs), (whole,) * 3)

    if aligned:
        one = ((tok, head), bf16)
        key_rows, value_rows = call(
            functools.partial(total_kernel, planes, xs, window), (parts,), (one, one)
        )
    else:
        split = parts.reshape(planes, xs, window, rp, 2 * head).astype(f32).sum(axis=1)
        total = sum(jnp.roll(split[:, window - 1 - j], -j, axis=0) for j in range(window))
        total = total.reshape(tok, 2 * head).astype(bf16)
        key_rows, value_rows = total[:, 0:head], total[:, head:]
    return key_rows, value_rows, q_out, k_out, v_out


def solution(mesh):
    groups, ctx = mesh.devices.shape
    fine = Mesh(mesh.devices.reshape(groups, ctx // 2, 2), ("groups", "zx", "core"))
    rows = P(("groups", "zx", "core"), None)
    return jax.shard_map(
        body,
        mesh=fine,
        in_specs=(rows,) * 9 + (P("groups"),),
        out_specs=(rows,) * 5,
        check_vma=False,
    )
```

```python
import functools

import jax
import jax.numpy as jnp
from jax import lax
from jax.experimental import pallas as pl
from jax.experimental.pallas import tpu as pltpu
from jax.sharding import Mesh
from jax.sharding import PartitionSpec as P

very_low = -1e30
f32, bf16, i32 = jnp.float32, jnp.bfloat16, jnp.int32
DEC_ROWS = 16
VMEM = pl.BlockSpec(memory_space=pltpu.VMEM)
SMEM = pl.BlockSpec(memory_space=pltpu.SMEM)
HBM = pl.BlockSpec(memory_space=pltpu.HBM)


def nt(a, b):
    return lax.dot_general(a, b, (((1,), (1,)), ((), ())), preferred_element_type=f32)


def nn(a, b):
    return lax.dot_general(a, b, (((1,), (0,)), ((), ())), preferred_element_type=f32)


def tn(a, b):
    return lax.dot_general(a, b, (((0,), (0,)), ((), ())), preferred_element_type=f32)


def iota(shape, dim):
    return lax.broadcasted_iota(i32, shape, dim)


def quot(x, d):
    return ((x.astype(f32) + 0.5) * (1.0 / d)).astype(i32)


def run_starts(docs):
    counts = []
    for v in (1, 2, 3):
        hit = jnp.where(docs < v, 1.0, 0.0)
        total = jnp.sum(jnp.sum(hit, axis=0, keepdims=True), axis=1, keepdims=True)
        counts.append(total.astype(i32))
    return counts


def start_of(pos, bounds):
    start = jnp.zeros_like(pos)
    for b in bounds:
        start = jnp.maximum(start, jnp.where(pos >= b, b, 0))
    return start


def chunks(count, body):
    if count <= 8:
        for i in range(count):
            body(i)
    else:
        lax.fori_loop(0, count, lambda i, c: (body(i), c)[1], 0)


def at(i, size):
    return pl.ds(i * size if isinstance(i, int) else pl.multiple_of(i * size, size), size)


def sums(dec_row):
    span = dec_row.shape[1]
    col, row = iota((span, span), 0), iota((span, span), 1)
    c_col = jnp.sum(jnp.where(row <= col, dec_row, 0.0), axis=1, keepdims=True)
    c_row = jnp.sum(jnp.where(row == col, c_col, 0.0), axis=0, keepdims=True)
    return c_row, c_col


def pack_linear(heads, idx_ref, q_ref, k_ref, v_ref, dec_ref, outs):
    tok, head = q_ref.shape[0], q_ref.shape[1] // heads
    p = lax.rem(idx_ref[0], heads)
    for k in range(heads):
        h = p ^ k
        lanes = pl.ds(pl.multiple_of(h * head, head), head)
        out = outs[k]
        out[0:tok, :] = q_ref[:, lanes]
        out[tok : 2 * tok, :] = k_ref[:, lanes]
        out[2 * tok : 3 * tok, :] = v_ref[:, lanes]
        d = dec_ref[pl.ds(h, 1), :]
        hi = d.astype(bf16).astype(f32)
        mid = (d - hi).astype(bf16).astype(f32)
        low = d - hi - mid
        r = iota((DEC_ROWS, tok), 0)
        rows = jnp.where(r == 0, hi, jnp.where(r == 1, mid, jnp.where(r == 2, low, 0.0)))
        out[3 * tok : 3 * tok + DEC_ROWS, :] = rows.astype(bf16)


def pack_main(heads, planes, window, idx_ref, q_ref, k_ref, v_ref, o_ref, g_ref, out):
    tok, head = k_ref.shape
    rp, xs = tok // planes, heads // 2
    zx = lax.div(idx_ref[0], 2)
    wide = xs * planes * rp
    cols = []
    for a in range(heads):
        s = slice(a * head, (a + 1) * head)
        cols.append(jnp.sum(g_ref[:, s].astype(f32) * o_ref[:, s].astype(f32), axis=1, keepdims=True))
    r, lane = iota((tok, wide), 0), iota((tok, wide), 1) - zx * rp
    r8 = iota((8, wide), 0)
    for g in range(planes):
        hit = (lane == r - g * rp) & (lane >= 0) & (lane < rp)
        rows = [jnp.sum(jnp.where(hit, c, 0.0), axis=0, keepdims=True) for c in cols]
        for x in range(xs):
            to = g * xs + x
            s = slice(x * 2 * head, (x + 1) * 2 * head)
            out[to, 0:rp, :] = q_ref[g * rp : (g + 1) * rp, s]
            out[to, rp : 2 * rp, :] = g_ref[g * rp : (g + 1) * rp, s]
            for w in range(window):
                plane = (g - window + 1 + w) % planes
                rows_w = slice((2 + w) * rp, (3 + w) * rp)
                out[to, rows_w, 0:head] = k_ref[plane * rp : (plane + 1) * rp, :]
                out[to, rows_w, head : 2 * head] = v_ref[plane * rp : (plane + 1) * rp, :]
            d0, d1 = rows[2 * x], rows[2 * x + 1]
            h0, h1 = d0.astype(bf16).astype(f32), d1.astype(bf16).astype(f32)
            tail = jnp.where(r8 == 0, h0, jnp.where(r8 == 1, d0 - h0, jnp.where(r8 == 2, h1, jnp.where(r8 == 3, d1 - h1, 0.0))))
            out[to, (2 + window) * rp : (2 + window) * rp + 8, :] = tail.astype(bf16)


def pack_kernel(heads, planes, window, count, idx_ref, *refs):
    ins, outs, held, sem = refs[:count], refs[count : -count - 1], refs[-count - 1 : -1], refs[-1]
    copies = [pltpu.make_async_copy(a, b, sem.at[i]) for i, (a, b) in enumerate(zip(ins, held))]
    for c in copies:
        c.start()
    for c in copies[-4:]:
        c.wait()
    pack_linear(heads, idx_ref, *held[-4:], outs[-heads:])
    if window:
        for c in copies[:-4]:
            c.wait()
        pack_main(heads, planes, window, idx_ref, *held[:5], outs[0])


def pack_main_plain(heads, planes, window, idx, q, k, v, o, grad):
    tok, head = k.shape
    rp, xs = tok // planes, heads // 2
    zx = idx[0] // 2
    wide = xs * planes * rp

    def pieces(a):
        return a.reshape(planes, rp, xs, 2 * head).swapaxes(1, 2).reshape(planes * xs, rp, 2 * head)

    kv = jnp.concatenate([k, v], axis=1).reshape(planes, rp, 2 * head)
    win = jnp.stack([jnp.roll(kv, window - 1 - w, axis=0) for w in range(window)], axis=1)
    win = jnp.repeat(win.reshape(planes, 1, window * rp, 2 * head), xs, axis=1)
    win = win.reshape(planes * xs, window * rp, 2 * head)
    delta = jnp.sum((grad.astype(f32) * o.astype(f32)).reshape(tok, heads, head), axis=-1)
    high = lax.reduce_precision(delta, 8, 7)
    parts = jnp.stack([high, delta - high], axis=-1).astype(bf16)
    parts = parts.reshape(planes, rp, xs, 4).transpose(0, 2, 3, 1).reshape(planes * xs, 4, rp)
    tail = jnp.zeros((planes * xs, 8, wide), bf16)
    tail = lax.dynamic_update_slice(tail, parts, (0, 0, zx * rp))
    return jnp.concatenate([pieces(q), pieces(grad), win, tail], axis=1)


def gather_linear(heads, idx_ref, docs_ref, *rest):
    msgs, (qkv, dec, state) = rest[:heads], rest[heads:]
    tok, head = (msgs[0].shape[0] - DEC_ROWS) // 3, msgs[0].shape[1]
    p, g = lax.rem(idx_ref[0], heads), lax.div(idx_ref[0], heads)
    span = heads * tok
    for k in range(heads):
        off = pl.multiple_of((p ^ k) * tok, tok)
        for j in range(3):
            qkv[j, pl.ds(off, tok), :] = msgs[k][j * tok : (j + 1) * tok, :]
        parts = msgs[k][3 * tok : 3 * tok + DEC_ROWS, :].astype(f32)
        dec[:, pl.ds(off, tok)] = jnp.broadcast_to(jnp.sum(parts, axis=0, keepdims=True), (8, tok))
    bounds = run_starts(docs_ref[...])
    dec_row = dec[0:1, :]
    _, c_col = sums(dec_row)
    total = jnp.sum(dec_row, axis=1, keepdims=True)
    pos = g * span + iota((span, 1), 0)
    last = start_of(jnp.zeros((1, 1), i32) + (g * span + span - 1), bounds)
    tail = jnp.where(pos >= last, jnp.exp(jnp.minimum(total - c_col, 0.0)), 0.0)
    weighted = (qkv[2].astype(f32) * tail).astype(bf16)
    state[0:head, :] = tn(weighted, qkv[1])
    state[head : head + 8, :] = jnp.broadcast_to(total, (8, head))


def softmax_kernel(cfg, *refs):
    heads, planes, window, tok, aligned = cfg
    if aligned:
        idx_ref, docs_ref, own, other, qkv, dec, keep, give, stream_out, state, s_scr, p_scr, ds_scr = refs
    else:
        idx_ref, docs_ref, q_in, g_in, kv_in, delta_in, qkv, dec, keep, give, stream_out, state, s_scr, p_scr, ds_scr = refs
    head = keep.shape[1] // 2
    rp, owners = tok // planes, heads * planes // 2
    n = 2 * owners
    half_keys = owners * window * rp
    keys, span = 2 * half_keys, heads * tok
    scale = head ** (-0.5)
    me = idx_ref[0]
    core, g = lax.rem(me, 2), lax.div(me, heads)
    bounds = run_starts(docs_ref[...])

    if aligned:
        mine = pl.ds(pl.multiple_of(core * head, head), head)
        kv_rows = slice(2 * rp, (2 + window) * rp)

        def both(rows, lanes):
            count = owners * (rows.stop - rows.start)
            return jnp.concatenate([ref[:, rows, lanes].reshape(count, head) for ref in (own, other)], axis=0)

        q = both(slice(0, rp), mine)
        grad = both(slice(rp, 2 * rp), mine)
        key = both(kv_rows, slice(0, head))
        value = both(kv_rows, slice(head, 2 * head))
        tails = []
        for ref in (own, other):
            t = jnp.zeros((8, owners * rp), f32)
            for o in range(owners):
                t = t + ref[o, (2 + window) * rp : (2 + window) * rp + 8, :].astype(f32)
            tails.append(jnp.where(core == 0, t[0:1] + t[1:2], t[2:3] + t[3:4]))
        delta = jnp.concatenate(tails, axis=1)
    else:
        q, grad = q_in[...], g_in[...]
        key, value = kv_in[:, 0:head], kv_in[:, head : 2 * head]
        delta = delta_in[0:1, :]

    j = iota((1, span), 1)
    side = quot(j, owners * rp)
    inner = j - side * (owners * rp)
    zx = quot(inner, rp)
    q_rel = (inner - zx * rp) * n + zx * 2 + jnp.where(side == 0, core, 1 - core)
    q_pos = q_rel + g * span
    q_start = start_of(q_pos, bounds)

    def key_pos(first, count):
        j = iota((count, 1), 0) + first
        side = jnp.where(j >= half_keys, 1, 0)
        inner = j - side * half_keys
        zx = quot(inner, window * rp)
        row = inner - zx * (window * rp) + (g - window + 1) * rp
        row = jnp.where(row < 0, row + tok, row)
        return row * n + zx * 2 + jnp.where(side == 0, core, 1 - core)

    if aligned:
        wide, deep = 256, 256
    else:
        wide, deep = 128, 256
    steps = keys // deep
    for b in range(span // wide):
        lanes = slice(b * wide, (b + 1) * wide)
        qb, gb = q[lanes, :], grad[lanes, :]
        lo, hi, db = q_start[:, lanes], q_pos[:, lanes], delta[:, lanes]

        def first(i, best):
            rows = at(i, deep)
            kc = key[i * deep : (i + 1) * deep] if aligned else kv_in[rows, 0:head]
            s = nt(kc, qb)
            pos = key_pos(i * deep, deep)
            s = jnp.where((pos >= lo) & (pos <= hi), s, very_low)
            s_scr[rows, :] = s
            return jnp.maximum(best, jnp.max(s.reshape(deep // 8, 8, wide), axis=0))

        def second(i, acc):
            rows = at(i, deep)
            e = jnp.exp((s_scr[rows, :] - best) * scale)
            s_scr[rows, :] = e
            return acc + jnp.sum(e.reshape(deep // 8, 8, wide), axis=0)

        def third(i):
            rows = at(i, deep)
            vc = value[i * deep : (i + 1) * deep] if aligned else kv_in[rows, head : 2 * head]
            pr = s_scr[rows, :] * inv
            dp = nt(vc, gb)
            p_scr[rows, lanes] = pr.astype(bf16)
            ds_scr[rows, lanes] = (pr * (dp - db) * scale).astype(bf16)

        best = jnp.full((8, wide), very_low, f32)
        acc = jnp.zeros((8, wide), f32)
        if aligned:
            for i in range(steps):
                best = first(i, best)
            best = jnp.max(best, axis=0, keepdims=True)
            for i in range(steps):
                acc = second(i, acc)
            inv = 1.0 / jnp.sum(acc, axis=0, keepdims=True)
            for i in range(steps):
                third(i)
        else:
            best = jnp.max(lax.fori_loop(0, steps, first, best), axis=0, keepdims=True)
            inv = 1.0 / jnp.sum(lax.fori_loop(0, steps, second, acc), axis=0, keepdims=True)
            lax.fori_loop(0, steps, lambda i, c: (third(i), c)[1], 0)

    eye = jnp.where(iota((head, head), 0) == iota((head, head), 1), 1.0, 0.0).astype(bf16)
    dq_t = tn(key, ds_scr[...])
    stream_t = (nt(eye, grad) + dq_t).astype(bf16)
    order = jnp.where(iota((span, span), 0) == q_rel, 1.0, 0.0).astype(bf16)
    stream = nt(order, stream_t).astype(bf16)
    stream_out[...] = stream

    _, c_col = sums(dec[0:1, :])
    start = start_of(iota((span, 1), 0) + g * span, bounds)
    weight = jnp.where(start < g * span, jnp.exp(c_col), 0.0)
    state[0:head, :] = tn((stream.astype(f32) * weight).astype(bf16), qkv[0])
    state[head : head + 8, :] = jnp.broadcast_to(jnp.sum(dec[0:1, :], axis=1, keepdims=True), (8, head))

    for i, out in enumerate((keep, give)):
        rows = slice(i * half_keys, (i + 1) * half_keys)
        out[:, 0:head] = nn(ds_scr[rows, :], q).astype(out.dtype)
        out[:, head : 2 * head] = nn(p_scr[rows, :], grad).astype(out.dtype)


def joined(states, g, span, bounds, step):
    head = states[0].shape[1]
    one = jnp.zeros((1, 1), i32)
    total, passed = None, jnp.zeros((1, 1), f32)
    for k, ref in enumerate(states, 1):
        if step < 0:
            open_ = start_of(one + (g * span - 1), bounds) < (g - k + 1) * span
        else:
            open_ = start_of(one + ((g + k) * span - 1), bounds) < (g + 1) * span
        part = ref[0:head, :] * jnp.where(open_, jnp.exp(passed), 0.0)
        total = part if total is None else total + part
        passed = passed + ref[head : head + 1, 0:1]
    return total


def linear_kernel(heads, idx_ref, docs_ref, stream_ref, qkv, dec, *rest):
    states, (q_out, k_out, v_out, dm, mx) = rest[:-5], rest[-5:]
    span, head = stream_ref.shape
    g = lax.div(idx_ref[0], heads)
    bounds = run_starts(docs_ref[...])
    earlier = joined(states, g, span, bounds, -1)
    c_row, c_col = sums(dec[0:1, :])
    stream, query, key, value = stream_ref[...], qkv[0], qkv[1], qkv[2]
    t = iota((1, span), 1)
    lo = start_of(t + g * span, bounds) - g * span
    deep = 128
    for i in range(span // deep):
        rows = slice(i * deep, (i + 1) * deep)
        s = iota((deep, 1), 0) + i * deep
        ratio = jnp.minimum(c_row - c_col[rows], 0.0)
        decay = jnp.where((s <= t) & (s >= lo), jnp.exp(ratio), 0.0)
        dm[rows, :] = (decay * nt(value[rows], stream)).astype(bf16)
        mx[rows, :] = (decay * nt(key[rows], query)).astype(bf16)
    start = start_of(iota((span, 1), 0) + g * span, bounds)
    weight = jnp.where(start < g * span, jnp.exp(c_col), 0.0)
    q_out[...] = (tn(dm[...], key) + weight * nn(stream, earlier.astype(bf16))).astype(bf16)
    k_out[...] = nn(dm[...], query)
    v_out[...] = nn(mx[...], stream)


def finish_kernel(heads, idx_ref, docs_ref, q_ref, k_ref, v_ref, qkv, dec, *rest):
    states, outs, (k_scr, v_scr) = rest[: -2 - heads], rest[-2 - heads : -2], rest[-2:]
    span, head = q_ref.shape
    tok = span // heads
    p, g = lax.rem(idx_ref[0], heads), lax.div(idx_ref[0], heads)
    bounds = run_starts(docs_ref[...])
    later = joined(states, g, span, bounds, 1).astype(bf16)
    _, c_col = sums(dec[0:1, :])
    total = jnp.sum(dec[0:1, :], axis=1, keepdims=True)
    pos = g * span + iota((span, 1), 0)
    last = start_of(jnp.zeros((1, 1), i32) + (g * span + span - 1), bounds)
    tail = jnp.where(pos >= last, jnp.exp(jnp.minimum(total - c_col, 0.0)), 0.0)
    k_scr[...] = (k_ref[...] + tail * nn(qkv[2], later)).astype(bf16)
    v_scr[...] = (v_ref[...] + tail * nt(qkv[1], later)).astype(bf16)
    for k in range(heads):
        rows = pl.ds(pl.multiple_of((p ^ k) * tok, tok), tok)
        outs[k][0:tok, :] = q_ref[rows, :]
        outs[k][tok : 2 * tok, :] = k_scr[rows, :]
        outs[k][2 * tok : 3 * tok, :] = v_scr[rows, :]


def spread_kernel(heads, idx_ref, *rest):
    msgs, outs = rest[:heads], rest[heads:]
    tok, head = outs[0].shape[0], outs[0].shape[1] // heads
    p = lax.rem(idx_ref[0], heads)
    for k in range(heads):
        lanes = pl.ds(pl.multiple_of((p ^ k) * head, head), head)
        for j in range(3):
            outs[j][:, lanes] = msgs[k][j * tok : (j + 1) * tok, :]


def total_kernel(planes, xs, window, parts, k_out, v_out):
    tok, head = k_out.shape
    rp = tok // planes
    for q in range(planes):
        total = None
        for j in range(window):
            w = window - 1 - j
            for x in range(xs):
                part = parts[((q + j) % planes) * xs + x, w * rp : (w + 1) * rp, :].astype(f32)
                total = part if total is None else total + part
        rows = slice(q * rp, (q + 1) * rp)
        k_out[rows, :] = total[:, 0:head].astype(bf16)
        v_out[rows, :] = total[:, head : 2 * head].astype(bf16)


def call(body, ins, outs, scratch=(), flops=1 << 20, grant=8, space=VMEM):
    in_specs = [SMEM if a.dtype == i32 and a.ndim == 1 else space for a in ins]
    return pl.pallas_call(
        body,
        in_specs=in_specs,
        out_specs=tuple(VMEM for _ in outs),
        out_shape=tuple(jax.ShapeDtypeStruct(*o) for o in outs),
        scratch_shapes=list(scratch),
        compiler_params=pltpu.CompilerParams(vmem_limit_bytes=grant << 20),
        cost_estimate=pl.CostEstimate(flops=flops, bytes_accessed=1 << 20, transcendentals=0),
    )(*ins)


def body(
    softmax_query,
    softmax_key,
    softmax_value,
    softmax_output,
    upstream_grad,
    linear_query,
    linear_key,
    linear_value,
    linear_decay,
    document_ids,
):
    tok, head = softmax_key.shape
    heads = softmax_query.shape[1] // head
    n = lax.axis_size("zx") * lax.axis_size("core")
    planes, xs = n // heads, heads // 2
    rp = tok // planes
    window = min(planes, planes // 2 + 1)
    owners = n // 2
    span = heads * tok
    half_keys = owners * window * rp
    aligned = rp % 16 == 0
    me = (lax.axis_index("zx") * 2 + lax.axis_index("core")).astype(i32)
    idx = me.reshape(1)
    docs = document_ids.reshape(-1, 128)
    line = ("zx", "core")

    def swap(a, k):
        return lax.ppermute(a, line, [(i, i ^ k) for i in range(n)])

    def shift(a, k):
        pairs = [(i, i + k * heads) for i in range(n) if 0 <= i + k * heads < n]
        return lax.ppermute(a, line, pairs)

    msg = ((3 * tok + DEC_ROWS, head), bf16)
    packed = (softmax_query, softmax_key, softmax_value, softmax_output, upstream_grad)
    linear = (linear_query, linear_key, linear_value, linear_decay.T)
    if aligned:
        rows = (2 + window) * rp + 8
        send, *lin = call(
            functools.partial(pack_kernel, heads, planes, window, 9),
            (idx, *packed, *linear),
            (((owners, rows, 2 * head), bf16),) + (msg,) * heads,
            [pltpu.VMEM(a.shape, a.dtype) for a in (*packed, *linear)] + [pltpu.SemaphoreType.DMA((9,))],
            grant=58,
            space=HBM,
        )
    else:
        send = pack_main_plain(heads, planes, window, idx, *packed)
        lin = call(
            functools.partial(pack_kernel, heads, planes, 0, 4),
            (idx, *linear),
            (msg,) * heads,
            [pltpu.VMEM(a.shape, a.dtype) for a in linear] + [pltpu.SemaphoreType.DMA((4,))],
            grant=58,
            space=HBM,
        )
    own = lax.all_to_all(send, "zx", 0, 0, tiled=True)
    lin = [lin[0]] + [swap(lin[k], k) for k in range(1, heads)]

    state = ((head + 8, head), f32)
    qkv, dec, forward = call(
        functools.partial(gather_linear, heads),
        (idx, docs, *lin),
        (((3, span, head), bf16), ((8, span), f32), state),
    )
    own, forward = lax.optimization_barrier((own, forward))
    before = [shift(forward, k) for k in range(1, window)]
    other = swap(own, 1)

    if aligned:
        given = (own, other)
        wide = 256
    else:
        core = me % 2
        halves = [lax.dynamic_slice_in_dim(a, core * head, head, 2) for a in (own, other)]
        q = jnp.concatenate([a[:, 0:rp].reshape(owners * rp, head) for a in halves])
        grad = jnp.concatenate([a[:, rp : 2 * rp].reshape(owners * rp, head) for a in halves])
        kv = jnp.concatenate([a[:, 2 * rp : -8].reshape(half_keys, 2 * head) for a in (own, other)])
        tails = [jnp.sum(a[:, -8:].astype(f32), axis=0) for a in (own, other)]
        tails = jnp.concatenate(tails, axis=1)
        delta = jnp.where(core == 0, tails[0] + tails[1], tails[2] + tails[3])
        given = (q, grad, kv, jnp.broadcast_to(delta[None], (8, span)))
        wide = 128
    keep, give, stream, backward = call(
        functools.partial(softmax_kernel, (heads, planes, window, tok, aligned)),
        (idx, docs, *given, qkv, dec),
        (((half_keys, 2 * head), f32), ((half_keys, 2 * head), bf16), ((span, head), bf16), state),
        [
            pltpu.VMEM((2 * half_keys, wide), f32),
            pltpu.VMEM((2 * half_keys, span), bf16),
            pltpu.VMEM((2 * half_keys, span), bf16),
        ],
        flops=1 << 30,
        grant=24 if aligned else 58,
    )
    taken = swap(give, 1)
    after = [shift(backward, -k) for k in range(1, window)]
    square = [pltpu.VMEM((span, span), bf16)] * 2
    q_cot, k_part, v_part = call(
        functools.partial(linear_kernel, heads),
        (idx, docs, stream, qkv, dec, *before),
        (((span, head), bf16), ((span, head), f32), ((span, head), f32)),
        square,
        flops=1 << 28,
        grant=16,
    )
    taken, k_part, *after = lax.optimization_barrier((taken, k_part, *after))
    parts = (keep + taken.astype(f32)).astype(bf16).reshape(owners, window * rp, 2 * head)
    parts = lax.all_to_all(parts, "zx", 0, 0, tiled=True)

    out = ((3 * tok, head), bf16)
    msgs = call(
        functools.partial(finish_kernel, heads),
        (idx, docs, q_cot, k_part, v_part, qkv, dec, *after),
        (out,) * heads,
        [pltpu.VMEM((span, head), bf16)] * 2,
    )
    msgs = [msgs[0]] + [swap(msgs[k], k) for k in range(1, heads)]
    whole = ((tok, heads * head), bf16)
    q_out, k_out, v_out = call(functools.partial(spread_kernel, heads), (idx, *msgs), (whole,) * 3)

    if aligned:
        one = ((tok, head), bf16)
        key_rows, value_rows = call(
            functools.partial(total_kernel, planes, xs, window), (parts,), (one, one)
        )
    else:
        split = parts.reshape(planes, xs, window, rp, 2 * head).astype(f32).sum(axis=1)
        total = sum(jnp.roll(split[:, window - 1 - j], -j, axis=0) for j in range(window))
        total = total.reshape(tok, 2 * head).astype(bf16)
        key_rows, value_rows = total[:, 0:head], total[:, head:]
    return key_rows, value_rows, q_out, k_out, v_out


def solution(mesh):
    groups, ctx = mesh.devices.shape
    fine = Mesh(mesh.devices.reshape(groups, ctx // 2, 2), ("groups", "zx", "core"))
    rows = P(("groups", "zx", "core"), None)
    return jax.shard_map(
        body,
        mesh=fine,
        in_specs=(rows,) * 9 + (P("groups"),),
        out_specs=(rows,) * 5,
        check_vma=False,
    )
```

```python
import functools

import jax
import jax.numpy as jnp
from jax import lax
from jax.experimental import pallas as pl
from jax.experimental.pallas import tpu as pltpu
from jax.sharding import Mesh
from jax.sharding import PartitionSpec as P

very_low = -1e30
f32, bf16, i32 = jnp.float32, jnp.bfloat16, jnp.int32
DEC_ROWS = 16
VMEM = pl.BlockSpec(memory_space=pltpu.VMEM)
SMEM = pl.BlockSpec(memory_space=pltpu.SMEM)
HBM = pl.BlockSpec(memory_space=pltpu.HBM)


def nt(a, b):
    return lax.dot_general(a, b, (((1,), (1,)), ((), ())), preferred_element_type=f32)


def nn(a, b):
    return lax.dot_general(a, b, (((1,), (0,)), ((), ())), preferred_element_type=f32)


def tn(a, b):
    return lax.dot_general(a, b, (((0,), (0,)), ((), ())), preferred_element_type=f32)


def iota(shape, dim):
    return lax.broadcasted_iota(i32, shape, dim)


def quot(x, d):
    return ((x.astype(f32) + 0.5) * (1.0 / d)).astype(i32)


def run_starts(docs):
    counts = []
    for v in (1, 2, 3):
        hit = jnp.where(docs < v, 1.0, 0.0)
        total = jnp.sum(jnp.sum(hit, axis=0, keepdims=True), axis=1, keepdims=True)
        counts.append(total.astype(i32))
    return counts


def start_of(pos, bounds):
    start = jnp.zeros_like(pos)
    for b in bounds:
        start = jnp.maximum(start, jnp.where(pos >= b, b, 0))
    return start


def chunks(count, body):
    if count <= 8:
        for i in range(count):
            body(i)
    else:
        lax.fori_loop(0, count, lambda i, c: (body(i), c)[1], 0)


def at(i, size):
    return pl.ds(i * size if isinstance(i, int) else pl.multiple_of(i * size, size), size)


def sums(dec_row):
    span = dec_row.shape[1]
    col, row = iota((span, span), 0), iota((span, span), 1)
    c_col = jnp.sum(jnp.where(row <= col, dec_row, 0.0), axis=1, keepdims=True)
    c_row = jnp.sum(jnp.where(row == col, c_col, 0.0), axis=0, keepdims=True)
    return c_row, c_col


def pack_linear(heads, idx_ref, q_ref, k_ref, v_ref, dec_ref, outs):
    tok, head = q_ref.shape[0], q_ref.shape[1] // heads
    p = lax.rem(idx_ref[0], heads)
    for k in range(heads):
        h = p ^ k
        lanes = pl.ds(pl.multiple_of(h * head, head), head)
        out = outs[k]
        out[0:tok, :] = q_ref[:, lanes]
        out[tok : 2 * tok, :] = k_ref[:, lanes]
        out[2 * tok : 3 * tok, :] = v_ref[:, lanes]
        d = dec_ref[pl.ds(h, 1), :]
        hi = d.astype(bf16).astype(f32)
        mid = (d - hi).astype(bf16).astype(f32)
        low = d - hi - mid
        r = iota((DEC_ROWS, tok), 0)
        rows = jnp.where(r == 0, hi, jnp.where(r == 1, mid, jnp.where(r == 2, low, 0.0)))
        out[3 * tok : 3 * tok + DEC_ROWS, :] = rows.astype(bf16)


def pack_main(heads, planes, window, idx_ref, q_ref, k_ref, v_ref, o_ref, g_ref, out):
    tok, head = k_ref.shape
    rp, xs = tok // planes, heads // 2
    zx = lax.div(idx_ref[0], 2)
    wide = xs * planes * rp
    cols = []
    for a in range(heads):
        s = slice(a * head, (a + 1) * head)
        cols.append(jnp.sum(g_ref[:, s].astype(f32) * o_ref[:, s].astype(f32), axis=1, keepdims=True))
    r, lane = iota((tok, wide), 0), iota((tok, wide), 1) - zx * rp
    r8 = iota((8, wide), 0)
    for g in range(planes):
        hit = (lane == r - g * rp) & (lane >= 0) & (lane < rp)
        rows = [jnp.sum(jnp.where(hit, c, 0.0), axis=0, keepdims=True) for c in cols]
        for x in range(xs):
            to = g * xs + x
            s = slice(x * 2 * head, (x + 1) * 2 * head)
            out[to, 0:rp, :] = q_ref[g * rp : (g + 1) * rp, s]
            out[to, rp : 2 * rp, :] = g_ref[g * rp : (g + 1) * rp, s]
            for w in range(window):
                plane = (g - window + 1 + w) % planes
                rows_w = slice((2 + w) * rp, (3 + w) * rp)
                out[to, rows_w, 0:head] = k_ref[plane * rp : (plane + 1) * rp, :]
                out[to, rows_w, head : 2 * head] = v_ref[plane * rp : (plane + 1) * rp, :]
            d0, d1 = rows[2 * x], rows[2 * x + 1]
            h0, h1 = d0.astype(bf16).astype(f32), d1.astype(bf16).astype(f32)
            tail = jnp.where(r8 == 0, h0, jnp.where(r8 == 1, d0 - h0, jnp.where(r8 == 2, h1, jnp.where(r8 == 3, d1 - h1, 0.0))))
            out[to, (2 + window) * rp : (2 + window) * rp + 8, :] = tail.astype(bf16)


def pack_kernel(heads, planes, window, count, idx_ref, *refs):
    ins, outs, held, sem = refs[:count], refs[count : -count - 1], refs[-count - 1 : -1], refs[-1]
    copies = [pltpu.make_async_copy(a, b, sem.at[i]) for i, (a, b) in enumerate(zip(ins, held))]
    for c in copies:
        c.start()
    for c in copies[-4:]:
        c.wait()
    pack_linear(heads, idx_ref, *held[-4:], outs[-heads:])
    if window:
        for c in copies[:-4]:
            c.wait()
        pack_main(heads, planes, window, idx_ref, *held[:5], outs[0])


def pack_main_plain(heads, planes, window, idx, q, k, v, o, grad):
    tok, head = k.shape
    rp, xs = tok // planes, heads // 2
    zx = idx[0] // 2
    wide = xs * planes * rp

    def pieces(a):
        return a.reshape(planes, rp, xs, 2 * head).swapaxes(1, 2).reshape(planes * xs, rp, 2 * head)

    kv = jnp.concatenate([k, v], axis=1).reshape(planes, rp, 2 * head)
    win = jnp.stack([jnp.roll(kv, window - 1 - w, axis=0) for w in range(window)], axis=1)
    win = jnp.repeat(win.reshape(planes, 1, window * rp, 2 * head), xs, axis=1)
    win = win.reshape(planes * xs, window * rp, 2 * head)
    delta = jnp.sum((grad.astype(f32) * o.astype(f32)).reshape(tok, heads, head), axis=-1)
    high = lax.reduce_precision(delta, 8, 7)
    parts = jnp.stack([high, delta - high], axis=-1).astype(bf16)
    parts = parts.reshape(planes, rp, xs, 4).transpose(0, 2, 3, 1).reshape(planes * xs, 4, rp)
    tail = jnp.zeros((planes * xs, 8, wide), bf16)
    tail = lax.dynamic_update_slice(tail, parts, (0, 0, zx * rp))
    return jnp.concatenate([pieces(q), pieces(grad), win, tail], axis=1)


def gather_linear(heads, idx_ref, docs_ref, *rest):
    msgs, (qkv, dec, state) = rest[:heads], rest[heads:]
    tok, head = (msgs[0].shape[0] - DEC_ROWS) // 3, msgs[0].shape[1]
    p, g = lax.rem(idx_ref[0], heads), lax.div(idx_ref[0], heads)
    span = heads * tok
    for k in range(heads):
        off = pl.multiple_of((p ^ k) * tok, tok)
        for j in range(3):
            qkv[j, pl.ds(off, tok), :] = msgs[k][j * tok : (j + 1) * tok, :]
        parts = msgs[k][3 * tok : 3 * tok + DEC_ROWS, :].astype(f32)
        dec[:, pl.ds(off, tok)] = jnp.broadcast_to(jnp.sum(parts, axis=0, keepdims=True), (8, tok))
    bounds = run_starts(docs_ref[...])
    dec_row = dec[0:1, :]
    _, c_col = sums(dec_row)
    total = jnp.sum(dec_row, axis=1, keepdims=True)
    pos = g * span + iota((span, 1), 0)
    last = start_of(jnp.zeros((1, 1), i32) + (g * span + span - 1), bounds)
    tail = jnp.where(pos >= last, jnp.exp(jnp.minimum(total - c_col, 0.0)), 0.0)
    weighted = (qkv[2].astype(f32) * tail).astype(bf16)
    state[0:head, :] = tn(weighted, qkv[1])
    state[head : head + 8, :] = jnp.broadcast_to(total, (8, head))


def softmax_kernel(cfg, *refs):
    heads, planes, window, tok, aligned = cfg
    if aligned:
        idx_ref, docs_ref, own, other, qkv, dec, keep, give, stream_out, state, s_scr, p_scr, ds_scr = refs
    else:
        idx_ref, docs_ref, q_in, g_in, kv_in, delta_in, qkv, dec, keep, give, stream_out, state, s_scr, p_scr, ds_scr = refs
    head = keep.shape[1] // 2
    rp, owners = tok // planes, heads * planes // 2
    n = 2 * owners
    half_keys = owners * window * rp
    keys, span = 2 * half_keys, heads * tok
    scale = head ** (-0.5)
    me = idx_ref[0]
    core, g = lax.rem(me, 2), lax.div(me, heads)
    bounds = run_starts(docs_ref[...])

    if aligned:
        mine = pl.ds(pl.multiple_of(core * head, head), head)
        kv_rows = slice(2 * rp, (2 + window) * rp)

        def both(rows, lanes):
            count = owners * (rows.stop - rows.start)
            return jnp.concatenate([ref[:, rows, lanes].reshape(count, head) for ref in (own, other)], axis=0)

        q = both(slice(0, rp), mine)
        grad = both(slice(rp, 2 * rp), mine)
        key = both(kv_rows, slice(0, head))
        value = both(kv_rows, slice(head, 2 * head))
        tails = []
        for ref in (own, other):
            t = jnp.zeros((8, owners * rp), f32)
            for o in range(owners):
                t = t + ref[o, (2 + window) * rp : (2 + window) * rp + 8, :].astype(f32)
            tails.append(jnp.where(core == 0, t[0:1] + t[1:2], t[2:3] + t[3:4]))
        delta = jnp.concatenate(tails, axis=1)
    else:
        q, grad = q_in[...], g_in[...]
        key, value = kv_in[:, 0:head], kv_in[:, head : 2 * head]
        delta = delta_in[0:1, :]

    j = iota((1, span), 1)
    side = quot(j, owners * rp)
    inner = j - side * (owners * rp)
    zx = quot(inner, rp)
    q_rel = (inner - zx * rp) * n + zx * 2 + jnp.where(side == 0, core, 1 - core)
    q_pos = q_rel + g * span
    q_start = start_of(q_pos, bounds)

    def key_pos(first, count):
        j = iota((count, 1), 0) + first
        side = jnp.where(j >= half_keys, 1, 0)
        inner = j - side * half_keys
        zx = quot(inner, window * rp)
        row = inner - zx * (window * rp) + (g - window + 1) * rp
        row = jnp.where(row < 0, row + tok, row)
        return row * n + zx * 2 + jnp.where(side == 0, core, 1 - core)

    if aligned:
        wide, deep = 256, 256
    else:
        wide, deep = 128, 256
    steps = keys // deep
    for b in range(span // wide):
        lanes = slice(b * wide, (b + 1) * wide)
        qb, gb = q[lanes, :], grad[lanes, :]
        lo, hi, db = q_start[:, lanes], q_pos[:, lanes], delta[:, lanes]

        def first(i, best):
            rows = at(i, deep)
            kc = key[i * deep : (i + 1) * deep] if aligned else kv_in[rows, 0:head]
            s = nt(kc, qb)
            pos = key_pos(i * deep, deep)
            s = jnp.where((pos >= lo) & (pos <= hi), s, very_low)
            s_scr[rows, :] = s
            return jnp.maximum(best, jnp.max(s.reshape(deep // 8, 8, wide), axis=0))

        def second(i, acc):
            rows = at(i, deep)
            e = jnp.exp((s_scr[rows, :] - best) * scale)
            s_scr[rows, :] = e
            return acc + jnp.sum(e.reshape(deep // 8, 8, wide), axis=0)

        def third(i):
            rows = at(i, deep)
            vc = value[i * deep : (i + 1) * deep] if aligned else kv_in[rows, head : 2 * head]
            pr = s_scr[rows, :] * inv
            dp = nt(vc, gb)
            p_scr[rows, lanes] = pr.astype(bf16)
            ds_scr[rows, lanes] = (pr * (dp - db) * scale).astype(bf16)

        best = jnp.full((8, wide), very_low, f32)
        acc = jnp.zeros((8, wide), f32)
        if aligned:
            for i in range(steps):
                best = first(i, best)
            best = jnp.max(best, axis=0, keepdims=True)
            for i in range(steps):
                acc = second(i, acc)
            inv = 1.0 / jnp.sum(acc, axis=0, keepdims=True)
            for i in range(steps):
                third(i)
        else:
            best = jnp.max(lax.fori_loop(0, steps, first, best), axis=0, keepdims=True)
            inv = 1.0 / jnp.sum(lax.fori_loop(0, steps, second, acc), axis=0, keepdims=True)
            lax.fori_loop(0, steps, lambda i, c: (third(i), c)[1], 0)

    eye = jnp.where(iota((head, head), 0) == iota((head, head), 1), 1.0, 0.0).astype(bf16)
    dq_t = tn(key, ds_scr[...])
    stream_t = (nt(eye, grad) + dq_t).astype(bf16)
    order = jnp.where(iota((span, span), 0) == q_rel, 1.0, 0.0).astype(bf16)
    stream = nt(order, stream_t).astype(bf16)
    stream_out[...] = stream

    _, c_col = sums(dec[0:1, :])
    start = start_of(iota((span, 1), 0) + g * span, bounds)
    weight = jnp.where(start < g * span, jnp.exp(c_col), 0.0)
    state[0:head, :] = tn((stream.astype(f32) * weight).astype(bf16), qkv[0])
    state[head : head + 8, :] = jnp.broadcast_to(jnp.sum(dec[0:1, :], axis=1, keepdims=True), (8, head))

    for i, out in enumerate((keep, give)):
        rows = slice(i * half_keys, (i + 1) * half_keys)
        out[:, 0:head] = nn(ds_scr[rows, :], q).astype(out.dtype)
        out[:, head : 2 * head] = nn(p_scr[rows, :], grad).astype(out.dtype)


def joined(states, g, span, bounds, step, positions):
    head = states[0].shape[1]
    one = jnp.zeros((1, 1), i32)
    total, passed = None, jnp.zeros((1, 1), f32)
    for k, ref in enumerate(states, 1):
        if step < 0:
            open_ = start_of(one + (g * span - 1), bounds) < (g - k + 1) * span
        else:
            limit = jnp.where((g + k) * span < positions, (g + 1) * span, 0)
            open_ = start_of(one + ((g + k) * span - 1), bounds) < limit
        part = ref[0:head, :] * jnp.where(open_, jnp.exp(passed), 0.0)
        total = part if total is None else total + part
        passed = passed + ref[head : head + 1, 0:1]
    return total


def linear_kernel(heads, idx_ref, docs_ref, stream_ref, qkv, dec, *rest):
    states, (q_out, k_out, v_out, dm, mx) = rest[:-5], rest[-5:]
    span, head = stream_ref.shape
    g = lax.div(idx_ref[0], heads)
    bounds = run_starts(docs_ref[...])
    earlier = joined(states, g, span, bounds, -1, docs_ref.size)
    c_row, c_col = sums(dec[0:1, :])
    stream, query, key, value = stream_ref[...], qkv[0], qkv[1], qkv[2]
    t = iota((1, span), 1)
    lo = start_of(t + g * span, bounds) - g * span
    deep = 128
    for i in range(span // deep):
        rows = slice(i * deep, (i + 1) * deep)
        s = iota((deep, 1), 0) + i * deep
        ratio = jnp.minimum(c_row - c_col[rows], 0.0)
        decay = jnp.where((s <= t) & (s >= lo), jnp.exp(ratio), 0.0)
        dm[rows, :] = (decay * nt(value[rows], stream)).astype(bf16)
        mx[rows, :] = (decay * nt(key[rows], query)).astype(bf16)
    start = start_of(iota((span, 1), 0) + g * span, bounds)
    weight = jnp.where(start < g * span, jnp.exp(c_col), 0.0)
    q_out[...] = (tn(dm[...], key) + weight * nn(stream, earlier.astype(bf16))).astype(bf16)
    k_out[...] = nn(dm[...], query)
    v_out[...] = nn(mx[...], stream)


def finish_kernel(heads, idx_ref, docs_ref, q_ref, k_ref, v_ref, qkv, dec, *rest):
    states, outs, (k_scr, v_scr) = rest[: -2 - heads], rest[-2 - heads : -2], rest[-2:]
    span, head = q_ref.shape
    tok = span // heads
    p, g = lax.rem(idx_ref[0], heads), lax.div(idx_ref[0], heads)
    bounds = run_starts(docs_ref[...])
    later = joined(states, g, span, bounds, 1, docs_ref.size).astype(bf16)
    _, c_col = sums(dec[0:1, :])
    total = jnp.sum(dec[0:1, :], axis=1, keepdims=True)
    pos = g * span + iota((span, 1), 0)
    last = start_of(jnp.zeros((1, 1), i32) + (g * span + span - 1), bounds)
    tail = jnp.where(pos >= last, jnp.exp(jnp.minimum(total - c_col, 0.0)), 0.0)
    k_scr[...] = (k_ref[...] + tail * nn(qkv[2], later)).astype(bf16)
    v_scr[...] = (v_ref[...] + tail * nt(qkv[1], later)).astype(bf16)
    for k in range(heads):
        rows = pl.ds(pl.multiple_of((p ^ k) * tok, tok), tok)
        outs[k][0:tok, :] = q_ref[rows, :]
        outs[k][tok : 2 * tok, :] = k_scr[rows, :]
        outs[k][2 * tok : 3 * tok, :] = v_scr[rows, :]


def spread_kernel(heads, idx_ref, *rest):
    msgs, outs = rest[:heads], rest[heads:]
    tok, head = outs[0].shape[0], outs[0].shape[1] // heads
    p = lax.rem(idx_ref[0], heads)
    for k in range(heads):
        lanes = pl.ds(pl.multiple_of((p ^ k) * head, head), head)
        for j in range(3):
            outs[j][:, lanes] = msgs[k][j * tok : (j + 1) * tok, :]


def total_kernel(planes, xs, window, parts, k_out, v_out):
    tok, head = k_out.shape
    rp = tok // planes
    for q in range(planes):
        total = None
        for j in range(window):
            w = window - 1 - j
            for x in range(xs):
                part = parts[((q + j) % planes) * xs + x, w * rp : (w + 1) * rp, :].astype(f32)
                total = part if total is None else total + part
        rows = slice(q * rp, (q + 1) * rp)
        k_out[rows, :] = total[:, 0:head].astype(bf16)
        v_out[rows, :] = total[:, head : 2 * head].astype(bf16)


def call(body, ins, outs, scratch=(), flops=1 << 20, grant=8, space=VMEM):
    in_specs = [SMEM if a.dtype == i32 and a.ndim == 1 else space for a in ins]
    return pl.pallas_call(
        body,
        in_specs=in_specs,
        out_specs=tuple(VMEM for _ in outs),
        out_shape=tuple(jax.ShapeDtypeStruct(*o) for o in outs),
        scratch_shapes=list(scratch),
        compiler_params=pltpu.CompilerParams(vmem_limit_bytes=grant << 20),
        cost_estimate=pl.CostEstimate(flops=flops, bytes_accessed=1 << 20, transcendentals=0),
    )(*ins)


def body(
    softmax_query,
    softmax_key,
    softmax_value,
    softmax_output,
    upstream_grad,
    linear_query,
    linear_key,
    linear_value,
    linear_decay,
    document_ids,
):
    tok, head = softmax_key.shape
    heads = softmax_query.shape[1] // head
    n = lax.axis_size("zx") * lax.axis_size("core")
    planes, xs = n // heads, heads // 2
    rp = tok // planes
    window = min(planes, planes // 2 + 1)
    owners = n // 2
    span = heads * tok
    half_keys = owners * window * rp
    aligned = rp % 16 == 0
    me = (lax.axis_index("zx") * 2 + lax.axis_index("core")).astype(i32)
    idx = me.reshape(1)
    docs = document_ids.reshape(-1, 128)
    line = ("zx", "core")

    def swap(a, k):
        return lax.ppermute(a, line, [(i, i ^ k) for i in range(n)])

    def ring(a, k):
        pairs = []
        for i in range(n):
            to = i // heads + k
            if (k if to < planes else planes - k) < window:
                pairs.append((i, (i + k * heads) % n))
        return lax.ppermute(a, line, pairs)

    msg = ((3 * tok + DEC_ROWS, head), bf16)
    packed = (softmax_query, softmax_key, softmax_value, softmax_output, upstream_grad)
    linear = (linear_query, linear_key, linear_value, linear_decay.T)
    if aligned:
        rows = (2 + window) * rp + 8
        send, *lin = call(
            functools.partial(pack_kernel, heads, planes, window, 9),
            (idx, *packed, *linear),
            (((owners, rows, 2 * head), bf16),) + (msg,) * heads,
            [pltpu.VMEM(a.shape, a.dtype) for a in (*packed, *linear)] + [pltpu.SemaphoreType.DMA((9,))],
            grant=58,
            space=HBM,
        )
    else:
        send = pack_main_plain(heads, planes, window, idx, *packed)
        lin = call(
            functools.partial(pack_kernel, heads, planes, 0, 4),
            (idx, *linear),
            (msg,) * heads,
            [pltpu.VMEM(a.shape, a.dtype) for a in linear] + [pltpu.SemaphoreType.DMA((4,))],
            grant=58,
            space=HBM,
        )
    own = lax.all_to_all(send, "zx", 0, 0, tiled=True)
    lin = [lin[0]] + [swap(lin[k], k) for k in range(1, heads)]

    state = ((head + 8, head), f32)
    qkv, dec, forward = call(
        functools.partial(gather_linear, heads),
        (idx, docs, *lin),
        (((3, span, head), bf16), ((8, span), f32), state),
    )
    own, forward = lax.optimization_barrier((own, forward))
    other = swap(own, 1)

    if aligned:
        given = (own, other)
        wide = 256
    else:
        core = me % 2
        halves = [lax.dynamic_slice_in_dim(a, core * head, head, 2) for a in (own, other)]
        q = jnp.concatenate([a[:, 0:rp].reshape(owners * rp, head) for a in halves])
        grad = jnp.concatenate([a[:, rp : 2 * rp].reshape(owners * rp, head) for a in halves])
        kv = jnp.concatenate([a[:, 2 * rp : -8].reshape(half_keys, 2 * head) for a in (own, other)])
        tails = [jnp.sum(a[:, -8:].astype(f32), axis=0) for a in (own, other)]
        tails = jnp.concatenate(tails, axis=1)
        delta = jnp.where(core == 0, tails[0] + tails[1], tails[2] + tails[3])
        given = (q, grad, kv, jnp.broadcast_to(delta[None], (8, span)))
        wide = 128
    keep, give, stream, backward = call(
        functools.partial(softmax_kernel, (heads, planes, window, tok, aligned)),
        (idx, docs, *given, qkv, dec),
        (((half_keys, 2 * head), f32), ((half_keys, 2 * head), bf16), ((span, head), bf16), state),
        [
            pltpu.VMEM((2 * half_keys, wide), f32),
            pltpu.VMEM((2 * half_keys, span), bf16),
            pltpu.VMEM((2 * half_keys, span), bf16),
        ],
        flops=1 << 30,
        grant=24 if aligned else 58,
    )
    taken = swap(give, 1)
    quarter = me // heads
    rings = [ring(jnp.where(quarter + k < planes, forward, backward), k) for k in range(1, planes)]
    before, after = rings[: window - 1], rings[::-1][: window - 1]
    square = [pltpu.VMEM((span, span), bf16)] * 2
    q_cot, k_part, v_part = call(
        functools.partial(linear_kernel, heads),
        (idx, docs, stream, qkv, dec, *before),
        (((span, head), bf16), ((span, head), f32), ((span, head), f32)),
        square,
        flops=1 << 28,
        grant=16,
    )
    taken, k_part, *after = lax.optimization_barrier((taken, k_part, *after))
    parts = (keep + taken.astype(f32)).astype(bf16).reshape(owners, window * rp, 2 * head)
    parts = lax.all_to_all(parts, "zx", 0, 0, tiled=True)

    out = ((3 * tok, head), bf16)
    msgs = call(
        functools.partial(finish_kernel, heads),
        (idx, docs, q_cot, k_part, v_part, qkv, dec, *after),
        (out,) * heads,
        [pltpu.VMEM((span, head), bf16)] * 2,
    )
    msgs = [msgs[0]] + [swap(msgs[k], k) for k in range(1, heads)]
    whole = ((tok, heads * head), bf16)
    q_out, k_out, v_out = call(functools.partial(spread_kernel, heads), (idx, *msgs), (whole,) * 3)

    if aligned:
        one = ((tok, head), bf16)
        key_rows, value_rows = call(
            functools.partial(total_kernel, planes, xs, window), (parts,), (one, one)
        )
    else:
        split = parts.reshape(planes, xs, window, rp, 2 * head).astype(f32).sum(axis=1)
        total = sum(jnp.roll(split[:, window - 1 - j], -j, axis=0) for j in range(window))
        total = total.reshape(tok, 2 * head).astype(bf16)
        key_rows, value_rows = total[:, 0:head], total[:, head:]
    return key_rows, value_rows, q_out, k_out, v_out


def solution(mesh):
    groups, ctx = mesh.devices.shape
    fine = Mesh(mesh.devices.reshape(groups, ctx // 2, 2), ("groups", "zx", "core"))
    rows = P(("groups", "zx", "core"), None)
    return jax.shard_map(
        body,
        mesh=fine,
        in_specs=(rows,) * 9 + (P("groups"),),
        out_specs=(rows,) * 5,
        check_vma=False,
    )
```
